512 devices in a mesh: ch: 32 (over z, core), lat: 4 (over y), lon: 4 (over x).
Axes of the slice: x: 4, y: 4, z: 16, core: 2. Of those that a mesh axis runs over, the one named last changes fastest.
Arguments:
- inputs: bfloat16 [512, 4, 16, 192], P('ch', None, 'lat', 'lon'), may hold values from -6 to 6
- weights: bfloat16 [512, 27, 512], P('ch'), may hold values from -0.0546875 to 0.0546875
- out_grad: bfloat16 [512, 4, 16, 192], P('ch', None, 'lat', 'lon'), may hold values from -6 to 6
Outputs:
- input_grad: bfloat16 [512, 4, 16, 192], P('ch', None, 'lat', 'lon')
- weight_grad: float32 [512, 27, 512], P('ch')
The draws below stay inside these ranges and needn't reach their ends.
All inputs are finite; a program needn't handle non-finite values.
Results may differ from the reference program's by a relative error of at most 0.001.
Values may be sent and summed in bfloat16 or wider, within the bound.
A program may use at most 64 MiB of HBM per device.

```python
import math
import jax
import jax.numpy as jnp

C = 512
F = 512
LEV = 4
NLON = 192
NLAT = 16


def block_scale(rng, shape, shards, low, largest):
    gain, own = 1.0, jax.random.fold_in(rng, 6)
    for axis_at, parts in shards:
        draws = jnp.exp(jax.random.uniform(jax.random.fold_in(own, axis_at), (parts,), jnp.float32, low / len(shards), largest / len(shards)))
        gain = gain * jnp.repeat(draws, shape[axis_at] // parts).reshape([-1 if axis == axis_at else 1 for axis in range(len(shape))])
    return gain


def scatter_about(rng, dims, scale, most, shards=(), kind=jnp.bfloat16):
    level = block_scale(rng, dims, shards, -0.22, 0.18) if shards else 1.0
    values = jax.random.normal(rng, dims, jnp.float32) * scale * level
    return jnp.minimum(jnp.maximum(values, -most), most).astype(kind)


def setup_inputs(seed: int = 0) -> dict:
    splits = jax.random.split(jax.random.key(seed), 4)
    inputs = scatter_about(splits[0], (C, LEV, NLAT, NLON), 1.0, 6.0, ((0, 32), (2, 4), (3, 4)))
    weights = scatter_about(splits[1], (C, 27, F), (27 * C) ** -0.5, 0.0546875, ((0, 32),))
    out_grad = scatter_about(splits[2], (F, LEV, NLAT, NLON), 1.0, 6.0, ((0, 32), (2, 4), (3, 4)))
    return {"inputs": inputs, "weights": weights, "out_grad": out_grad}


def pad_field(field):
    field = jnp.concatenate([field[..., -1:], field, field[..., :1]], axis=3)
    return jnp.pad(field, ((0, 0), (1, 1), (1, 1), (0, 0)))

def reference(inputs, weights, out_grad):
    input_pad = pad_field(inputs.astype(jnp.float32))
    grad_pad = pad_field(out_grad.astype(jnp.float32))
    grad_full = out_grad.astype(jnp.float32)
    taps = weights.astype(jnp.float32)
    levels, height, width = (inputs.shape[1], inputs.shape[2], inputs.shape[3])
    total = jnp.zeros(inputs.shape, jnp.float32)
    pieces = []
    for tap in range(27):
        shift_lev = tap // 9 - 1
        shift_lat = tap // 3 % 3 - 1
        shift_lon = tap % 3 - 1
        shifted = grad_pad[:, 1 - shift_lev:1 - shift_lev + levels, 1 - shift_lat:1 - shift_lat + height, 1 - shift_lon:1 - shift_lon + width]
        total = total + jnp.einsum('cf,flhw->clhw', taps[:, tap, :], shifted)
        moved = input_pad[:, 1 + shift_lev:1 + shift_lev + levels, 1 + shift_lat:1 + shift_lat + height, 1 + shift_lon:1 + shift_lon + width]
        pieces.append(jnp.einsum('clhw,flhw->cf', moved, grad_full))
    raw = jnp.stack(pieces, axis=1)
    weight_grad = raw * (1.0 / math.sqrt(LEV * NLAT * NLON))
    return (total.astype(jnp.bfloat16), weight_grad)
```

```python
import math

import jax
import jax.numpy as jnp
from jax import lax
from jax.experimental import pallas as pl
from jax.experimental.pallas import tpu as pltpu
from jax.sharding import PartitionSpec as P

MESH = pl.DeviceIdType.MESH
F32 = jnp.float32
BF16 = jnp.bfloat16

CH = 16
LEV = 4
ROWS = 4
COLS = 48
GROUPS = ROWS * LEV
CELLS = GROUPS * COLS
HALF = CELLS // 2
SIDE = 4
TAPS = 27
PER = 7
PART = 56
FILT = 512
STEP_LAT = LEV * COLS
NEAR = [(a, b) for a in (-1, 0, 1) for b in (-1, 0, 1) if (a, b) != (0, 0)]


def roll(values, shift):
    return pltpu.roll(values, shift % values.shape[1], axis=1)


def iota(shape, dim):
    return lax.broadcasted_iota(jnp.int32, shape, dim)


def group_of(lane):
    return lax.shift_right_logical(lane * 1366, 16)


def lane_places(rows):
    lane = iota((rows, CELLS), 1)
    group = group_of(lane)
    return lax.shift_right_logical(group, 2), group & 3, lane - group * COLS


def spread_matrix():
    lane = iota((COLS, CELLS), 1)
    return jnp.where(lane - group_of(lane) * COLS == iota((COLS, CELLS), 0), 1.0, 0.0).astype(BF16)


def keep_matrix():
    row = iota((GROUPS, CELLS), 0)
    group = (row & 3) * 4 + lax.shift_right_logical(row, 2)
    return jnp.where(group_of(iota((GROUPS, CELLS), 1)) == group, 1.0, 0.0).astype(F32)


def to_lanes(block, spread, keep):
    wide = jnp.dot(block, spread, preferred_element_type=F32).reshape(CH, GROUPS, CELLS)
    wide = (wide * keep[None]).reshape(CH * GROUPS, CELLS).astype(BF16)
    shape = (CH, CH * GROUPS)
    pick = jnp.where(lax.shift_right_logical(iota(shape, 1), 4) == iota(shape, 0), 1.0, 0.0).astype(BF16)
    return jnp.dot(pick, wide, preferred_element_type=F32).astype(BF16)


def from_lanes(cells, spread, keep):
    shape = (CH * GROUPS, CH)
    pick = jnp.where(lax.shift_right_logical(iota(shape, 0), 4) == iota(shape, 1), 1.0, 0.0).astype(BF16)
    wide = jnp.dot(pick, cells, preferred_element_type=F32).reshape(CH, GROUPS, CELLS)
    wide = (wide * keep[None]).reshape(CH * GROUPS, CELLS).astype(BF16)
    return lax.dot_general(
        wide, spread, (((1,), (1,)), ((), ())), preferred_element_type=F32
    ).astype(BF16)


def moved_row(near, d_lat, places):
    row, _, _ = places
    moved = {}
    for b in (-1, 0, 1):
        if d_lat == 0:
            moved[b] = near(0, b)
        elif d_lat == 1:
            moved[b] = roll(jnp.where(row == 0, near(1, b), near(0, b)), -STEP_LAT)
        else:
            moved[b] = roll(jnp.where(row == ROWS - 1, near(-1, b), near(0, b)), STEP_LAT)
    return moved


def taps_of_row(moved, places):
    _, level, col = places
    for d_lon in (-1, 0, 1):
        if d_lon == 0:
            base = moved[0]
        elif d_lon == 1:
            base = jnp.where(col == COLS - 1, roll(moved[1], COLS - 1), roll(moved[0], -1))
        else:
            base = jnp.where(col == 0, roll(moved[-1], 1 - COLS), roll(moved[0], 1))
        yield 0, d_lon, base
        yield 1, d_lon, jnp.where(level < LEV - 1, roll(base, -COLS), 0.0)
        yield -1, d_lon, jnp.where(level > 0, roll(base, COLS), 0.0)


def shifted_sums(product, places):
    row, level, col = places
    own = {}
    east = {}
    west = {}
    for d_lat in (-1, 0, 1):
        q = {}
        for d_lon in (-1, 0, 1):
            tap = (d_lat + 1) * 3 + d_lon + 1
            q[d_lon] = (
                product(9 + tap)
                + jnp.where(level > 0, roll(product(18 + tap), COLS), 0.0)
                + jnp.where(level < LEV - 1, roll(product(tap), -COLS), 0.0)
            )
        own[d_lat] = (
            q[0]
            + jnp.where(col > 0, roll(q[1], 1), 0.0)
            + jnp.where(col < COLS - 1, roll(q[-1], -1), 0.0)
        )
        east[d_lat] = jnp.where(col == 0, roll(q[1], 1 - COLS), 0.0)
        west[d_lat] = jnp.where(col == COLS - 1, roll(q[-1], COLS - 1), 0.0)
    out = {}
    for b, sums in ((0, own), (1, east), (-1, west)):
        up = roll(sums[1], STEP_LAT)
        down = roll(sums[-1], -STEP_LAT)
        out[0, b] = (
            sums[0] + jnp.where(row > 0, up, 0.0) + jnp.where(row < ROWS - 1, down, 0.0)
        )
        out[1, b] = jnp.where(row == 0, up, 0.0)
        out[-1, b] = jnp.where(row == ROWS - 1, down, 0.0)
    return out


def pack_column(frame):
    low = frame[:, 0:128] + frame[:, 128:256] + frame[:, 256:384]
    high = frame[:, 384:512] + frame[:, 512:640] + frame[:, 640:768]
    return low + roll(high, 1)


def unpack_column(packed, places, at):
    other = roll(packed, -1)
    wide = jnp.concatenate([packed] * 3 + [other] * 3, axis=1)
    return jnp.where(places[2] == at, wide, 0.0)


def kernel(
    nz,
    scale,
    x_ref,
    w_hbm,
    g_ref,
    xg_ref,
    wg_ref,
    field,
    cols,
    gath,
    wts,
    prod,
    part,
    slab,
    got1,
    got2,
    full,
    lat_out,
    lat_in,
    pt_out,
    pt_in,
    w_sem,
    ring_send,
    ring_recv,
    sib_send,
    sib_recv,
    xh_send,
    xh_recv,
    ph_send,
    ph_recv,
    st_send,
    st_recv,
):
    ch = lax.axis_index("ch")
    lat = lax.axis_index("lat")
    lon = lax.axis_index("lon")
    z = ch // 2
    core = ch % 2
    sibling = z * 2 + (1 - core)
    here = {"lat": lat, "lon": lon}

    def z_at(step):
        return lax.rem(z + step + nz, nz) * 2 + core

    def side_at(axis, step):
        return lax.rem(here[axis] + step + SIDE, SIDE)

    fetch = pltpu.make_async_copy(w_hbm, wts, w_sem)
    fetch.start()

    barrier = pltpu.get_barrier_semaphore()
    peers = [{"ch": z_at(1)}, {"ch": z_at(-1)}, {"ch": sibling}]
    for axis in ("lat", "lon"):
        peers += [{axis: side_at(axis, step)} for step in (1, 2, 3)]
    peers += [
        {"lat": side_at("lat", a), "lon": side_at("lon", b)} for a in (-1, 1) for b in (-1, 1)
    ]
    for peer in peers:
        pl.semaphore_signal(barrier, inc=1, device_id=peer, device_id_type=MESH)

    places = lane_places(CH)
    spread = spread_matrix()
    keep = keep_matrix()
    gath[ch] = to_lanes(g_ref[...], spread, keep)
    field[4] = to_lanes(x_ref[...], spread, keep)

    pl.semaphore_wait(barrier, len(peers))

    sends = []

    def send(src, dst, send_sem, recv_sem, peer):
        copy = pltpu.make_async_remote_copy(
            src_ref=src,
            dst_ref=dst,
            send_sem=send_sem,
            recv_sem=recv_sem,
            device_id=peer,
            device_id_type=MESH,
        )
        copy.start()
        sends.append(copy)

    def arrived(dst, send_sem, recv_sem, peer):
        pltpu.make_async_remote_copy(
            src_ref=dst,
            dst_ref=dst,
            send_sem=send_sem,
            recv_sem=recv_sem,
            device_id=peer,
            device_id_type=MESH,
        ).wait_recv()

    def onward(way, step):
        sign = 1 if way == 0 else -1
        slot = z_at(-sign * (step - 1))
        send(
            gath.at[slot],
            gath.at[slot],
            ring_send.at[way, step - 1],
            ring_recv.at[way, step - 1],
            {"ch": z_at(sign)},
        )

    def across(order, step):
        slot = z_at(step)
        send(gath.at[slot], gath.at[slot], sib_send.at[order], sib_recv.at[order], {"ch": sibling})

    reach = (nz // 2, (nz - 1) // 2)

    onward(0, 1)
    onward(1, 1)
    across(0, 0)
    for n, (a, b) in enumerate(NEAR):
        send(
            field.at[4],
            field.at[(1 - a) * 3 + 1 - b],
            xh_send.at[n],
            xh_recv.at[n],
            {"lat": side_at("lat", a), "lon": side_at("lon", b)},
        )

    south = jnp.where(lat > 0, 1.0, 0.0).astype(F32)
    north = jnp.where(lat < SIDE - 1, 1.0, 0.0).astype(F32)
    inside = {-1: south, 1: north}

    def near(a, b):
        block = field[(a + 1) * 3 + b + 1].astype(F32)
        return block if a == 0 else block * inside[a]

    def build(d_lat):
        for d_lev, d_lon, value in taps_of_row(moved_row(near, d_lat, places), places):
            tap = (d_lev + 1) * 9 + (d_lat + 1) * 3 + d_lon + 1
            value = value.astype(BF16)
            for side in range(2):
                at = (tap // PER * 2 + side) * PART + tap % PER * 8
                cols[at : at + 8, :] = value[side * 8 : side * 8 + 8]

    def clear_spare():
        for side in range(2):
            at = (3 * 2 + side) * PART + 6 * 8
            cols[at : at + 8, :] = jnp.zeros((8, CELLS), BF16)

    def wait_field():
        for n, (a, b) in enumerate(NEAR):
            arrived(
                field.at[(1 - a) * 3 + 1 - b],
                xh_send.at[n],
                xh_recv.at[n],
                {"lat": side_at("lat", -a), "lon": side_at("lon", -b)},
            )

    order = 1
    for step in range(1, reach[0] + 1):
        for way in (0, 1):
            if step > reach[way]:
                continue
            sign = 1 if way == 0 else -1
            slot = z_at(-sign * step)
            arrived(
                gath.at[slot],
                ring_send.at[way, step - 1],
                ring_recv.at[way, step - 1],
                {"ch": z_at(-sign)},
            )
            if step < reach[way]:
                onward(way, step + 1)
            across(order, -sign * step)
            order += 1
        if step == 1:
            clear_spare()
        if step == 2:
            wait_field()
            build(0)
        if step == 3:
            build(1)
        if step == 4:
            build(-1)
    order = 0
    for step in [0] + [s for n in range(1, reach[0] + 1) for s in (-n, n) if s != reach[0]]:
        slot = lax.rem(z + step + nz, nz) * 2 + (1 - core)
        arrived(gath.at[slot], sib_send.at[order], sib_recv.at[order], {"ch": sibling})
        order += 1

    axes = (("lat", "lon"), ("lon", "lat"))

    def sum_half(half):
        filters = gath[half * 16 : half * 16 + 16].reshape(FILT // 2, CELLS)
        sums = lax.dot_general(
            cols[...], filters, (((1,), (1,)), ((), ())), preferred_element_type=F32
        )
        for n in range(2):
            part[2 * half + n] = sums[:, n * 128 : n * 128 + 128].reshape(SIDE, 2, PART, 128)

    def stage_send(stage, half, src, dst):
        axis = axes[half][0 if stage in (0, 3) else 1]
        for d in (1, 3, 2):
            peer = side_at(axis, d)
            send(
                src(peer),
                dst(d - 1),
                st_send.at[stage, half, d - 1],
                st_recv.at[stage, half, d - 1],
                {axis: peer},
            )

    def stage_wait(stage, half, dst):
        axis = axes[half][0 if stage in (0, 3) else 1]
        for d in (1, 3, 2):
            peer = side_at(axis, -d)
            arrived(
                dst(d - 1, peer),
                st_send.at[stage, half, d - 1],
                st_recv.at[stage, half, d - 1],
                {axis: peer},
            )

    for half in range(2):
        sum_half(half)
        stage_send(
            0,
            half,
            lambda peer: part.at[pl.ds(2 * half, 2), peer],
            lambda n: got1.at[half, n],
        )

    fetch.wait()
    prod[...] = jnp.dot(
        wts[...].reshape(TAPS * CH, FILT),
        gath[...].reshape(FILT, CELLS),
        preferred_element_type=F32,
    )
    sums = shifted_sums(lambda tap: prod[tap * CH : tap * CH + CH, :], places)
    mine = sums[0, 0]
    lat_out[0] = sums[1, 0][:, 0:256]
    lat_out[1] = sums[-1, 0][:, CELLS - 256 : CELLS]
    columns = [(a, b) for a in (-1, 0, 1) for b in (-1, 1)]
    for n, at in enumerate(columns):
        pt_out[n] = pack_column(sums[at])
    prod[0:CH, :] = mine
    for n, a in enumerate((1, -1)):
        send(
            lat_out.at[n],
            lat_in.at[n],
            ph_send.at[n],
            ph_recv.at[n],
            {"lat": side_at("lat", a)},
        )
    for n, (a, b) in enumerate(columns):
        send(
            pt_out.at[n],
            pt_in.at[n],
            ph_send.at[2 + n],
            ph_recv.at[2 + n],
            {"lat": side_at("lat", a), "lon": side_at("lon", b)},
        )

    for half in range(2):
        first = here[axes[half][0]]
        stage_wait(0, half, lambda n, peer: got1.at[half, n])
        for v in range(SIDE):
            slab[half, v] = (
                part[2 * half + v // 2, first, v % 2]
                + got1[half, 0, v // 2, v % 2]
                + got1[half, 1, v // 2, v % 2]
                + got1[half, 2, v // 2, v % 2]
            )
        stage_send(
            1,
            half,
            lambda peer: slab.at[half, peer],
            lambda n: got2.at[half, n],
        )

    for n, a in enumerate((1, -1)):
        arrived(
            lat_in.at[n], ph_send.at[n], ph_recv.at[n], {"lat": side_at("lat", -a)}
        )
    for n, (a, b) in enumerate(columns):
        arrived(
            pt_in.at[n],
            ph_send.at[2 + n],
            ph_recv.at[2 + n],
            {"lat": side_at("lat", -a), "lon": side_at("lon", -b)},
        )
    total = prod[0:CH, :]
    total += jnp.concatenate(
        [lat_in[0] * south, jnp.zeros((CH, CELLS - 512), F32), lat_in[1] * north], axis=1
    )
    for n, (a, b) in enumerate(columns):
        packed = pt_in[n]
        if a != 0:
            packed = packed * (south if a == 1 else north)
        total += unpack_column(packed, places, 0 if b == 1 else COLS - 1)
    xg_ref[...] = from_lanes(total.astype(BF16), spread, keep)

    for half in range(2):
        first, second = here[axes[half][0]], here[axes[half][1]]
        stage_wait(1, half, lambda n, peer: got2.at[half, n])
        full[2 * half + second // 2, first, second % 2] = (
            slab[half, second] + got2[half, 0] + got2[half, 1] + got2[half, 2]
        ) * scale
        chunk = full.at[2 * half + second // 2, first, second % 2]
        stage_send(2, half, lambda peer: chunk, lambda n: chunk)
    for half in range(2):
        first = here[axes[half][0]]
        stage_wait(
            2, half, lambda n, peer: full.at[2 * half + peer // 2, first, peer % 2]
        )
        block = full.at[pl.ds(2 * half, 2), first]
        stage_send(3, half, lambda peer: block, lambda n: block)
    for half in range(2):
        stage_wait(3, half, lambda n, peer: full.at[pl.ds(2 * half, 2), peer])
    for tap in range(TAPS):
        for n in range(FILT // 128):
            for side in range(2):
                wg_ref[tap, side * 8 : side * 8 + 8, n * 128 : n * 128 + 128] = full[
                    n, tap // PER, side, tap % PER * 8 : tap % PER * 8 + 8, :
                ]
    for copy in sends:
        copy.wait_send()


def body(inputs, weights, out_grad):
    nz = lax.axis_size("ch") // 2
    cells = CELLS * lax.axis_size("lat") * lax.axis_size("lon")
    dma = pltpu.SemaphoreType.DMA
    vmem = pl.BlockSpec(memory_space=pltpu.VMEM)
    input_grad, weight_grad = pl.pallas_call(
        lambda *refs: kernel(nz, 1.0 / math.sqrt(cells), *refs),
        out_shape=(
            jax.ShapeDtypeStruct((CH * GROUPS, COLS), BF16),
            jax.ShapeDtypeStruct((TAPS, CH, FILT), F32),
        ),
        in_specs=[vmem, pl.BlockSpec(memory_space=pl.ANY), vmem],
        out_specs=(vmem, vmem),
        scratch_shapes=[
            pltpu.VMEM((9, CH, CELLS), BF16),
            pltpu.VMEM((SIDE * 2 * PART, CELLS), BF16),
            pltpu.VMEM((2 * nz, CH, CELLS), BF16),
            pltpu.VMEM((TAPS, CH, FILT), BF16),
            pltpu.VMEM((TAPS * CH, CELLS), F32),
            pltpu.VMEM((4, SIDE, 2, PART, 128), F32),
            pltpu.VMEM((2, SIDE, PART, 128), F32),
            pltpu.VMEM((2, 3, 2, 2, PART, 128), F32),
            pltpu.VMEM((2, 3, PART, 128), F32),
            pltpu.VMEM((4, SIDE, 2, PART, 128), F32),
            pltpu.VMEM((2, CH, 256), F32),
            pltpu.VMEM((2, CH, 256), F32),
            pltpu.VMEM((6, CH, 128), F32),
            pltpu.VMEM((6, CH, 128), F32),
            dma,
            dma((2, nz // 2)),
            dma((2, nz // 2)),
            dma((nz,)),
            dma((nz,)),
            dma((8,)),
            dma((8,)),
            dma((8,)),
            dma((8,)),
            dma((4, 2, 3)),
            dma((4, 2, 3)),
        ],
        compiler_params=pltpu.CompilerParams(
            collective_id=0, has_side_effects=True, vmem_limit_bytes=40 << 20
        ),
    )(
        inputs.reshape(CH * GROUPS, COLS),
        jnp.transpose(weights, (1, 0, 2)),
        out_grad.reshape(CH * GROUPS, COLS),
    )
    return input_grad.reshape(inputs.shape), jnp.transpose(weight_grad, (1, 0, 2))


def solution(mesh):
    in_specs = (P("ch", None, "lat", "lon"), P("ch", None, None), P("ch", None, "lat", "lon"))
    out_specs = (P("ch", None, "lat", "lon"), P("ch", None, None))
    return jax.shard_map(body, mesh=mesh, in_specs=in_specs, out_specs=out_specs, check_vma=False)
```

```python
import math

import jax
import jax.numpy as jnp
from jax import lax
from jax.experimental import pallas as pl
from jax.experimental.pallas import tpu as pltpu
from jax.sharding import PartitionSpec as P

MESH = pl.DeviceIdType.MESH
F32 = jnp.float32
BF16 = jnp.bfloat16

CH = 16
LEV = 4
ROWS = 4
COLS = 48
GROUPS = ROWS * LEV
CELLS = GROUPS * COLS
SIDE = 4
TAPS = 27
PER = 7
PART = PER * CH
FILT = 512
STEP_LAT = LEV * COLS
TOP = 2.0**30
TINY = 1e-28
VMEM_BYTES = 60 << 20
OTHERS = sorted(
    ((a, b) for a in range(SIDE) for b in range(SIDE) if (a, b) != (0, 0)),
    key=lambda at: -(min(at[0], SIDE - at[0]) + min(at[1], SIDE - at[1])),
)
NEAR = [(a, b) for a in (-1, 0, 1) for b in (-1, 0, 1) if (a, b) != (0, 0)]


def roll(values, shift):
    return pltpu.roll(values, shift % values.shape[1], axis=1)


def iota(shape, dim):
    return lax.broadcasted_iota(jnp.int32, shape, dim)


def group_of(lane):
    return lax.shift_right_logical(lane * 1366, 16)


def lane_places(rows):
    lane = iota((rows, CELLS), 1)
    group = group_of(lane)
    return lax.shift_right_logical(group, 2), group & 3, lane - group * COLS


def spread_matrix():
    lane = iota((COLS, CELLS), 1)
    return jnp.where(lane - group_of(lane) * COLS == iota((COLS, CELLS), 0), 1.0, 0.0).astype(BF16)


def keep_matrix():
    row = iota((GROUPS, CELLS), 0)
    group = (row & 3) * 4 + lax.shift_right_logical(row, 2)
    return jnp.where(group_of(iota((GROUPS, CELLS), 1)) == group, 1.0, 0.0).astype(F32)


def to_lanes(block, spread, keep):
    wide = jnp.dot(block, spread, preferred_element_type=F32).reshape(CH, GROUPS, CELLS)
    wide = (wide * keep[None]).reshape(CH * GROUPS, CELLS).astype(BF16)
    shape = (CH, CH * GROUPS)
    pick = jnp.where(lax.shift_right_logical(iota(shape, 1), 4) == iota(shape, 0), 1.0, 0.0).astype(BF16)
    return jnp.dot(pick, wide, preferred_element_type=F32).astype(BF16)


def from_lanes(cells, spread, keep):
    shape = (CH * GROUPS, CH)
    pick = jnp.where(lax.shift_right_logical(iota(shape, 0), 4) == iota(shape, 1), 1.0, 0.0).astype(BF16)
    wide = jnp.dot(pick, cells, preferred_element_type=F32).reshape(CH, GROUPS, CELLS)
    wide = (wide * keep[None]).reshape(CH * GROUPS, CELLS).astype(BF16)
    return lax.dot_general(
        wide, spread, (((1,), (1,)), ((), ())), preferred_element_type=F32
    ).astype(BF16)


def moved_row(near, d_lat, places):
    row, _, _ = places
    moved = {}
    for b in (-1, 0, 1):
        if d_lat == 0:
            moved[b] = near(0, b)
        elif d_lat == 1:
            moved[b] = roll(jnp.where(row == 0, near(1, b), near(0, b)), -STEP_LAT)
        else:
            moved[b] = roll(jnp.where(row == ROWS - 1, near(-1, b), near(0, b)), STEP_LAT)
    return moved


def taps_of_row(moved, places):
    _, level, col = places
    for d_lon in (-1, 0, 1):
        if d_lon == 0:
            base = moved[0]
        elif d_lon == 1:
            base = jnp.where(col == COLS - 1, roll(moved[1], COLS - 1), roll(moved[0], -1))
        else:
            base = jnp.where(col == 0, roll(moved[-1], 1 - COLS), roll(moved[0], 1))
        yield 0, d_lon, base
        yield 1, d_lon, jnp.where(level < LEV - 1, roll(base, -COLS), 0.0)
        yield -1, d_lon, jnp.where(level > 0, roll(base, COLS), 0.0)


def shifted_sums(product, places):
    row, level, col = places
    own = {}
    east = {}
    west = {}
    for d_lat in (-1, 0, 1):
        q = {}
        for d_lon in (-1, 0, 1):
            tap = (d_lat + 1) * 3 + d_lon + 1
            q[d_lon] = (
                product(9 + tap)
                + jnp.where(level > 0, roll(product(18 + tap), COLS), 0.0)
                + jnp.where(level < LEV - 1, roll(product(tap), -COLS), 0.0)
            )
        own[d_lat] = (
            q[0]
            + jnp.where(col > 0, roll(q[1], 1), 0.0)
            + jnp.where(col < COLS - 1, roll(q[-1], -1), 0.0)
        )
        east[d_lat] = jnp.where(col == 0, roll(q[1], 1 - COLS), 0.0)
        west[d_lat] = jnp.where(col == COLS - 1, roll(q[-1], COLS - 1), 0.0)
    out = {}
    for b, sums in ((0, own), (1, east), (-1, west)):
        up = roll(sums[1], STEP_LAT)
        down = roll(sums[-1], -STEP_LAT)
        out[0, b] = (
            sums[0] + jnp.where(row > 0, up, 0.0) + jnp.where(row < ROWS - 1, down, 0.0)
        )
        out[1, b] = jnp.where(row == 0, up, 0.0)
        out[-1, b] = jnp.where(row == ROWS - 1, down, 0.0)
    return out


def pack_column(frame):
    low = frame[:, 0:128] + frame[:, 128:256] + frame[:, 256:384]
    high = frame[:, 384:512] + frame[:, 512:640] + frame[:, 640:768]
    return low + roll(high, 1)


def unpack_column(packed, places, at):
    other = roll(packed, -1)
    wide = jnp.concatenate([packed] * 3 + [other] * 3, axis=1)
    return jnp.where(places[2] == at, wide, 0.0)


def encode(values, scale):
    scaled = values * scale
    square = scaled * scaled
    return (square * scaled * jnp.abs(scaled)).astype(BF16)


def decode(codes):
    inverse = 1.0 / codes[PART:, :].astype(F32)
    power = codes[:PART, :].astype(F32).reshape(PART // 8, 8, 128)
    root = lax.rsqrt(lax.rsqrt(jnp.abs(power))) * inverse[None]
    return jnp.where(power < 0, -root, root).reshape(PART, 128)


def scale_for(largest):
    return (TOP / jnp.maximum(largest, TINY)).astype(BF16)


def kernel(
    nz,
    scale,
    x_hbm,
    w_hbm,
    g_hbm,
    xg_ref,
    wg_ref,
    x_own,
    g_own,
    field,
    cols,
    gath,
    wts,
    prod,
    part,
    codes,
    got,
    full,
    lat_out,
    lat_in,
    pt_out,
    pt_in,
    in_sem,
    z_send,
    z_recv,
    sib_send,
    sib_recv,
    xh_send,
    xh_recv,
    ph_send,
    ph_recv,
    rs_send,
    rs_recv,
    ag_send,
    ag_recv,
):
    ch = lax.axis_index("ch")
    lat = lax.axis_index("lat")
    lon = lax.axis_index("lon")
    z = ch // 2
    core = ch % 2
    sibling = z * 2 + (1 - core)
    here = {"lat": lat, "lon": lon}

    fetches = [
        pltpu.make_async_copy(src, dst, in_sem.at[n])
        for n, (src, dst) in enumerate(((g_hbm, g_own), (x_hbm, x_own), (w_hbm, wts)))
    ]
    for fetch in fetches:
        fetch.start()

    def z_at(step):
        return lax.rem(z + step + nz, nz) * 2 + core

    def side_at(axis, step):
        return lax.rem(here[axis] + step + SIDE, SIDE)

    def plane_at(a, b):
        return {"lat": side_at("lat", a), "lon": side_at("lon", b)}

    barrier = pltpu.get_barrier_semaphore()
    peers = [{"ch": z_at(step)} for step in (4, -4, 3, -3, 2, -2, 1, -1)]
    peers += [{"ch": sibling}] + [plane_at(a, b) for a, b in OTHERS]
    for peer in peers:
        pl.semaphore_signal(barrier, inc=1, device_id=peer, device_id_type=MESH)

    places = lane_places(CH)
    spread = spread_matrix()
    keep = keep_matrix()
    fetches[0].wait()
    gath[ch] = to_lanes(g_own[...], spread, keep)
    fetches[1].wait()
    field[4] = to_lanes(x_own[...], spread, keep)

    pl.semaphore_wait(barrier, len(peers))

    sends = []

    def send(src, dst, send_sem, recv_sem, peer):
        copy = pltpu.make_async_remote_copy(
            src_ref=src,
            dst_ref=dst,
            send_sem=send_sem,
            recv_sem=recv_sem,
            device_id=peer,
            device_id_type=MESH,
        )
        copy.start()
        sends.append(copy)

    def arrived(dst, send_sem, recv_sem, peer):
        pltpu.make_async_remote_copy(
            src_ref=dst,
            dst_ref=dst,
            send_sem=send_sem,
            recv_sem=recv_sem,
            device_id=peer,
            device_id_type=MESH,
        ).wait_recv()

    def to_chip(dist, hop):
        slot = z_at(hop - dist)
        at = (dist + 7) % 16
        send(
            gath.at[slot],
            gath.at[slot],
            z_send.at[at],
            z_recv.at[at],
            {"ch": z_at(hop)},
        )

    def to_sibling(dist):
        slot = z_at(-dist)
        at = (dist + 7) % 16
        send(gath.at[slot], gath.at[slot], sib_send.at[at], sib_recv.at[at], {"ch": sibling})

    def block_here(dist, hop):
        at = (dist + 7) % 16
        arrived(gath.at[z_at(-dist)], z_send.at[at], z_recv.at[at], {"ch": z_at(-hop)})
        to_sibling(dist)

    for dist in (4, -4, 1, -1):
        to_chip(dist, dist)
    to_sibling(0)
    for n, (a, b) in enumerate(NEAR):
        send(
            field.at[4],
            field.at[(1 - a) * 3 + 1 - b],
            xh_send.at[n],
            xh_recv.at[n],
            plane_at(a, b),
        )

    south = jnp.where(lat > 0, 1.0, 0.0).astype(F32)
    north = jnp.where(lat < SIDE - 1, 1.0, 0.0).astype(F32)
    inside = {-1: south, 1: north}

    def near(a, b):
        block = field[(a + 1) * 3 + b + 1].astype(F32)
        return block if a == 0 else block * inside[a]

    def build(d_lat):
        for d_lev, d_lon, value in taps_of_row(moved_row(near, d_lat, places), places):
            tap = (d_lev + 1) * 9 + (d_lat + 1) * 3 + d_lon + 1
            cols[tap * CH : tap * CH + CH, :] = value.astype(BF16)

    cols[TAPS * CH :, :] = jnp.zeros((CH, CELLS), BF16)
    block_here(1, 1)
    to_chip(2, 1)
    block_here(-1, -1)
    to_chip(-2, -1)
    for n, (a, b) in enumerate(NEAR):
        arrived(
            field.at[(1 - a) * 3 + 1 - b], xh_send.at[n], xh_recv.at[n], plane_at(-a, -b)
        )
    build(0)
    block_here(4, 4)
    for hop in (3, 2, 1, -1):
        to_chip(4 + hop, hop)
    block_here(-4, -4)
    for hop in (-3, -2, -1, 1):
        to_chip(-4 + hop, hop)
    way = 4 - 8 * core
    far = z_at(-way)
    send(gath.at[far], gath.at[far], z_send.at[15], z_recv.at[15], {"ch": z_at(way)})
    build(1)
    build(-1)
    for dist, hop in ((2, 1), (-2, -1), (3, -1), (-3, 1), (5, 1), (-5, -1), (6, 2), (-6, -2)):
        block_here(dist, hop)
    for dist, hop in ((7, 3), (-7, -3)):
        block_here(dist, hop)
    block_here(8, way)
    for dist in (0, 1, -1, 4, -4, 2, -2, 3, -3, 5, -5, 6, -6, 7, -7, 8):
        slot = lax.rem(z - dist + nz, nz) * 2 + (1 - core)
        at = (dist + 7) % 16
        arrived(gath.at[slot], sib_send.at[at], sib_recv.at[at], {"ch": sibling})

    largest = None
    for half in range(2):
        filters = gath[half * 16 : half * 16 + 16].reshape(FILT // 2, CELLS)
        sums = lax.dot_general(
            cols[...], filters, (((1,), (1,)), ((), ())), preferred_element_type=F32
        )
        most = jnp.max(jnp.abs(sums), axis=0, keepdims=True)
        largest = most if largest is None else jnp.maximum(largest, most)
        for n in range(2):
            for a in range(SIDE):
                part[a * SIDE + 2 * half + n] = sums[
                    a * PART : a * PART + PART, n * 128 : n * 128 + 128
                ]
    factor = scale_for(jnp.max(largest, axis=1, keepdims=True))
    for n in range(SIDE * SIDE):
        codes[n, :PART, :] = encode(part[n], factor.astype(F32))
        codes[n, PART:, :] = jnp.broadcast_to(factor, (8, 128))
    for n, (a, b) in enumerate(OTHERS):
        peer = plane_at(a, b)
        send(
            codes.at[peer["lat"] * SIDE + peer["lon"]],
            got.at[n],
            rs_send.at[n],
            rs_recv.at[n],
            peer,
        )

    fetches[2].wait()
    prod[...] = jnp.dot(
        wts[...].reshape(TAPS * CH, FILT),
        gath[...].reshape(FILT, CELLS),
        preferred_element_type=F32,
    )
    sums = shifted_sums(lambda tap: prod[tap * CH : tap * CH + CH, :], places)
    mine = sums[0, 0]
    lat_out[0] = sums[1, 0][:, 0:256]
    lat_out[1] = sums[-1, 0][:, CELLS - 256 : CELLS]
    columns = [(a, b) for a in (-1, 0, 1) for b in (-1, 1)]
    for n, at in enumerate(columns):
        pt_out[n] = pack_column(sums[at])
    prod[0:CH, :] = mine
    for n, a in enumerate((1, -1)):
        send(lat_out.at[n], lat_in.at[n], ph_send.at[n], ph_recv.at[n], plane_at(a, 0))
    for n, (a, b) in enumerate(columns):
        send(pt_out.at[n], pt_in.at[n], ph_send.at[2 + n], ph_recv.at[2 + n], plane_at(a, b))

    mine_at = lat * SIDE + lon
    share = part[mine_at]
    for n, (a, b) in enumerate(OTHERS):
        arrived(got.at[n], rs_send.at[n], rs_recv.at[n], plane_at(-a, -b))
        share += decode(got[n])
    share *= scale
    factor = scale_for(jnp.max(jnp.max(jnp.abs(share), axis=0, keepdims=True), axis=1, keepdims=True))
    full[mine_at, :PART, :] = encode(share, factor.astype(F32))
    full[mine_at, PART:, :] = jnp.broadcast_to(factor, (8, 128))
    for n, (a, b) in enumerate(OTHERS):
        send(
            full.at[mine_at], full.at[mine_at], ag_send.at[n], ag_recv.at[n], plane_at(a, b)
        )

    for n, a in enumerate((1, -1)):
        arrived(lat_in.at[n], ph_send.at[n], ph_recv.at[n], plane_at(-a, 0))
    for n, (a, b) in enumerate(columns):
        arrived(pt_in.at[n], ph_send.at[2 + n], ph_recv.at[2 + n], plane_at(-a, -b))
    total = prod[0:CH, :]
    total += jnp.concatenate(
        [lat_in[0] * south, jnp.zeros((CH, CELLS - 512), F32), lat_in[1] * north], axis=1
    )
    for n, (a, b) in enumerate(columns):
        packed = pt_in[n]
        if a != 0:
            packed = packed * (south if a == 1 else north)
        total += unpack_column(packed, places, 0 if b == 1 else COLS - 1)
    xg_ref[...] = from_lanes(total.astype(BF16), spread, keep)

    def put(at_lat, at_lon):
        lanes = pl.ds(pl.multiple_of(at_lon * 128, 128), 128)
        wg_ref[pl.ds(at_lat * PER, PER), :, lanes] = decode(full[at_lat * SIDE + at_lon]).reshape(
            PER, CH, 128
        )

    put(lat, lon)
    for n, (a, b) in enumerate(OTHERS):
        peer = plane_at(-a, -b)
        arrived(
            full.at[peer["lat"] * SIDE + peer["lon"]], ag_send.at[n], ag_recv.at[n], peer
        )
        put(peer["lat"], peer["lon"])
    for copy in sends:
        copy.wait_send()


def body(inputs, weights, out_grad):
    nz = lax.axis_size("ch") // 2
    cells = CELLS * lax.axis_size("lat") * lax.axis_size("lon")
    dma = pltpu.SemaphoreType.DMA
    vmem = pl.BlockSpec(memory_space=pltpu.VMEM)
    whole = pl.BlockSpec(memory_space=pl.ANY)
    input_grad, weight_grad = pl.pallas_call(
        lambda *refs: kernel(nz, 1.0 / math.sqrt(cells), *refs),
        out_shape=(
            jax.ShapeDtypeStruct((CH * GROUPS, COLS), BF16),
            jax.ShapeDtypeStruct((SIDE * PER, CH, FILT), F32),
        ),
        in_specs=[whole] * 3,
        out_specs=(vmem, vmem),
        scratch_shapes=[
            pltpu.VMEM((CH * GROUPS, COLS), BF16),
            pltpu.VMEM((CH * GROUPS, COLS), BF16),
            pltpu.VMEM((9, CH, CELLS), BF16),
            pltpu.VMEM((SIDE * PART, CELLS), BF16),
            pltpu.VMEM((2 * nz, CH, CELLS), BF16),
            pltpu.VMEM((TAPS, CH, FILT), BF16),
            pltpu.VMEM((TAPS * CH, CELLS), F32),
            pltpu.VMEM((SIDE * SIDE, PART, 128), F32),
            pltpu.VMEM((SIDE * SIDE, PART + 8, 128), BF16),
            pltpu.VMEM((15, PART + 8, 128), BF16),
            pltpu.VMEM((SIDE * SIDE, PART + 8, 128), BF16),
            pltpu.VMEM((2, CH, 256), F32),
            pltpu.VMEM((2, CH, 256), F32),
            pltpu.VMEM((6, CH, 128), F32),
            pltpu.VMEM((6, CH, 128), F32),
            dma((3,)),
            dma((16,)),
            dma((16,)),
            dma((16,)),
            dma((16,)),
            dma((8,)),
            dma((8,)),
            dma((8,)),
            dma((8,)),
            dma((15,)),
            dma((15,)),
            dma((15,)),
            dma((15,)),
        ],
        compiler_params=pltpu.CompilerParams(
            collective_id=0, has_side_effects=True, vmem_limit_bytes=VMEM_BYTES
        ),
    )(
        inputs.reshape(CH * GROUPS, COLS),
        jnp.transpose(weights, (1, 0, 2)),
        out_grad.reshape(CH * GROUPS, COLS),
    )
    return input_grad.reshape(inputs.shape), jnp.transpose(weight_grad[:TAPS], (1, 0, 2))


def solution(mesh):
    in_specs = (P("ch", None, "lat", "lon"), P("ch", None, None), P("ch", None, "lat", "lon"))
    out_specs = (P("ch", None, "lat", "lon"), P("ch", None, None))
    return jax.shard_map(body, mesh=mesh, in_specs=in_specs, out_specs=out_specs, check_vma=False)
```

```python
import math

import jax
import jax.numpy as jnp
from jax import lax
from jax.experimental import pallas as pl
from jax.experimental.pallas import tpu as pltpu
from jax.sharding import PartitionSpec as P

MESH = pl.DeviceIdType.MESH
F32 = jnp.float32
BF16 = jnp.bfloat16

CH = 16
LEV = 4
ROWS = 4
COLS = 48
GROUPS = ROWS * LEV
CELLS = GROUPS * COLS
SIDE = 4
TAPS = 27
PER = 7
PART = PER * CH // 2
FILT = 512
STEP_LAT = LEV * COLS
TOP = 2.0**30
TINY = 1e-28
VMEM_BYTES = 24 << 20
OTHERS = sorted(
    ((a, b) for a in range(SIDE) for b in range(SIDE) if (a, b) != (0, 0)),
    key=lambda at: -(min(at[0], SIDE - at[0]) + min(at[1], SIDE - at[1])),
)
NEAR = [(a, b) for a in (-1, 0, 1) for b in (-1, 0, 1) if (a, b) != (0, 0)]


def roll(values, shift):
    return pltpu.roll(values, shift % values.shape[1], axis=1)


def iota(shape, dim):
    return lax.broadcasted_iota(jnp.int32, shape, dim)


def group_of(lane):
    return lax.shift_right_logical(lane * 1366, 16)


def lane_places(rows):
    lane = iota((rows, CELLS), 1)
    group = group_of(lane)
    return lax.shift_right_logical(group, 2), group & 3, lane - group * COLS


def spread_matrix():
    lane = iota((COLS, CELLS), 1)
    return jnp.where(lane - group_of(lane) * COLS == iota((COLS, CELLS), 0), 1.0, 0.0).astype(BF16)


def keep_matrix():
    row = iota((GROUPS, CELLS), 0)
    group = (row & 3) * 4 + lax.shift_right_logical(row, 2)
    return jnp.where(group_of(iota((GROUPS, CELLS), 1)) == group, 1.0, 0.0).astype(F32)


def to_lanes(block, spread, keep):
    wide = jnp.dot(block, spread, preferred_element_type=F32).reshape(CH, GROUPS, CELLS)
    wide = (wide * keep[None]).reshape(CH * GROUPS, CELLS).astype(BF16)
    shape = (CH, CH * GROUPS)
    pick = jnp.where(lax.shift_right_logical(iota(shape, 1), 4) == iota(shape, 0), 1.0, 0.0).astype(BF16)
    return jnp.dot(pick, wide, preferred_element_type=F32).astype(BF16)


def from_lanes(cells, spread, keep):
    shape = (CH * GROUPS, CH)
    pick = jnp.where(lax.shift_right_logical(iota(shape, 0), 4) == iota(shape, 1), 1.0, 0.0).astype(BF16)
    wide = jnp.dot(pick, cells, preferred_element_type=F32).reshape(CH, GROUPS, CELLS)
    wide = (wide * keep[None]).reshape(CH * GROUPS, CELLS).astype(BF16)
    return lax.dot_general(
        wide, spread, (((1,), (1,)), ((), ())), preferred_element_type=F32
    ).astype(BF16)


def moved_row(near, d_lat, places):
    row, _, _ = places
    moved = {}
    for b in (-1, 0, 1):
        if d_lat == 0:
            moved[b] = near(0, b)
        elif d_lat == 1:
            moved[b] = roll(jnp.where(row == 0, near(1, b), near(0, b)), -STEP_LAT)
        else:
            moved[b] = roll(jnp.where(row == ROWS - 1, near(-1, b), near(0, b)), STEP_LAT)
    return moved


def taps_of_row(moved, places):
    _, level, col = places
    for d_lon in (-1, 0, 1):
        if d_lon == 0:
            base = moved[0]
        elif d_lon == 1:
            base = jnp.where(col == COLS - 1, roll(moved[1], COLS - 1), roll(moved[0], -1))
        else:
            base = jnp.where(col == 0, roll(moved[-1], 1 - COLS), roll(moved[0], 1))
        yield 0, d_lon, base
        yield 1, d_lon, jnp.where(level < LEV - 1, roll(base, -COLS), 0.0)
        yield -1, d_lon, jnp.where(level > 0, roll(base, COLS), 0.0)


def shifted_sums(product, places):
    row, level, col = places
    own = {}
    east = {}
    west = {}
    for d_lat in (-1, 0, 1):
        q = {}
        for d_lon in (-1, 0, 1):
            tap = (d_lat + 1) * 3 + d_lon + 1
            q[d_lon] = (
                product(9 + tap)
                + jnp.where(level > 0, roll(product(18 + tap), COLS), 0.0)
                + jnp.where(level < LEV - 1, roll(product(tap), -COLS), 0.0)
            )
        own[d_lat] = (
            q[0]
            + jnp.where(col > 0, roll(q[1], 1), 0.0)
            + jnp.where(col < COLS - 1, roll(q[-1], -1), 0.0)
        )
        east[d_lat] = jnp.where(col == 0, roll(q[1], 1 - COLS), 0.0)
        west[d_lat] = jnp.where(col == COLS - 1, roll(q[-1], COLS - 1), 0.0)
    out = {}
    for b, sums in ((0, own), (1, east), (-1, west)):
        up = roll(sums[1], STEP_LAT)
        down = roll(sums[-1], -STEP_LAT)
        out[0, b] = (
            sums[0] + jnp.where(row > 0, up, 0.0) + jnp.where(row < ROWS - 1, down, 0.0)
        )
        out[1, b] = jnp.where(row == 0, up, 0.0)
        out[-1, b] = jnp.where(row == ROWS - 1, down, 0.0)
    return out


def pack_column(frame):
    low = frame[:, 0:128] + frame[:, 128:256] + frame[:, 256:384]
    high = frame[:, 384:512] + frame[:, 512:640] + frame[:, 640:768]
    return low + roll(high, 1)


def unpack_column(packed, places, at):
    other = roll(packed, -1)
    wide = jnp.concatenate([packed] * 3 + [other] * 3, axis=1)
    return jnp.where(places[2] == at, wide, 0.0)


def encode(values, scale):
    scaled = values * scale
    square = scaled * scaled
    return (square * scaled * jnp.abs(scaled)).astype(BF16)


def decode(codes):
    inverse = 1.0 / codes[PART:, :].astype(F32)
    power = codes[:PART, :].astype(F32).reshape(PART // 8, 8, 128)
    root = lax.rsqrt(lax.rsqrt(jnp.abs(power))) * inverse[None]
    return jnp.where(power < 0, -root, root).reshape(PART, 128)


def scale_for(largest):
    return (TOP / jnp.maximum(largest, TINY)).astype(BF16)


def kernel(
    nz,
    scale,
    x_hbm,
    w_hbm,
    g_hbm,
    xg_ref,
    wg_ref,
    x_own,
    g_own,
    field,
    cols,
    gath,
    wts,
    prod,
    part,
    codes,
    got,
    full,
    lat_out,
    lat_in,
    pt_out,
    pt_in,
    in_sem,
    z_send,
    z_recv,
    sib_send,
    sib_recv,
    xh_send,
    xh_recv,
    ph_send,
    ph_recv,
    rs_send,
    rs_recv,
    ag_send,
    ag_recv,
):
    ch = lax.axis_index("ch")
    lat = lax.axis_index("lat")
    lon = lax.axis_index("lon")
    z = ch // 2
    core = ch % 2
    sibling = z * 2 + (1 - core)
    here = {"lat": lat, "lon": lon}

    fetches = [
        pltpu.make_async_copy(src, dst, in_sem.at[n])
        for n, (src, dst) in enumerate(((g_hbm, g_own), (x_hbm, x_own), (w_hbm, wts)))
    ]
    for fetch in fetches:
        fetch.start()

    def z_at(step):
        return lax.rem(z + step + nz, nz) * 2 + core

    def side_at(axis, step):
        return lax.rem(here[axis] + step + SIDE, SIDE)

    def plane_at(a, b):
        return {"lat": side_at("lat", a), "lon": side_at("lon", b)}

    barrier = pltpu.get_barrier_semaphore()
    peers = [{"ch": z_at(step)} for step in (4, -4, 3, -3, 2, -2, 1, -1)]
    peers += [{"ch": sibling}] + [plane_at(a, b) for a, b in OTHERS]
    for peer in peers:
        pl.semaphore_signal(barrier, inc=1, device_id=peer, device_id_type=MESH)

    places = lane_places(CH)
    spread = spread_matrix()
    keep = keep_matrix()
    fetches[0].wait()
    gath[ch] = to_lanes(g_own[...], spread, keep)
    fetches[1].wait()
    field[4] = to_lanes(x_own[...], spread, keep)

    pl.semaphore_wait(barrier, len(peers))

    sends = []

    def send(src, dst, send_sem, recv_sem, peer):
        copy = pltpu.make_async_remote_copy(
            src_ref=src,
            dst_ref=dst,
            send_sem=send_sem,
            recv_sem=recv_sem,
            device_id=peer,
            device_id_type=MESH,
        )
        copy.start()
        sends.append(copy)

    def arrived(dst, send_sem, recv_sem, peer):
        pltpu.make_async_remote_copy(
            src_ref=dst,
            dst_ref=dst,
            send_sem=send_sem,
            recv_sem=recv_sem,
            device_id=peer,
            device_id_type=MESH,
        ).wait_recv()

    def to_chip(dist, hop):
        slot = z_at(hop - dist)
        at = (dist + 7) % 16
        send(
            gath.at[slot],
            gath.at[slot],
            z_send.at[at],
            z_recv.at[at],
            {"ch": z_at(hop)},
        )

    def to_sibling(dist):
        slot = z_at(-dist)
        at = (dist + 7) % 16
        send(gath.at[slot], gath.at[slot], sib_send.at[at], sib_recv.at[at], {"ch": sibling})

    def block_here(dist, hop):
        at = (dist + 7) % 16
        arrived(gath.at[z_at(-dist)], z_send.at[at], z_recv.at[at], {"ch": z_at(-hop)})
        to_sibling(dist)

    for dist in (4, -4, 1, -1):
        to_chip(dist, dist)
    to_sibling(0)
    for n, (a, b) in enumerate(NEAR):
        send(
            field.at[4],
            field.at[(1 - a) * 3 + 1 - b],
            xh_send.at[n],
            xh_recv.at[n],
            plane_at(a, b),
        )

    south = jnp.where(lat > 0, 1.0, 0.0).astype(F32)
    north = jnp.where(lat < SIDE - 1, 1.0, 0.0).astype(F32)
    inside = {-1: south, 1: north}

    def near(a, b):
        block = field[(a + 1) * 3 + b + 1].astype(F32)
        return block if a == 0 else block * inside[a]

    def build(d_lat):
        for d_lev, d_lon, value in taps_of_row(moved_row(near, d_lat, places), places):
            tap = (d_lev + 1) * 9 + (d_lat + 1) * 3 + d_lon + 1
            cols[tap * CH : tap * CH + CH, :] = value.astype(BF16)

    cols[TAPS * CH :, :] = jnp.zeros((CH, CELLS), BF16)
    block_here(1, 1)
    to_chip(2, 1)
    block_here(-1, -1)
    to_chip(-2, -1)
    for n, (a, b) in enumerate(NEAR):
        arrived(
            field.at[(1 - a) * 3 + 1 - b], xh_send.at[n], xh_recv.at[n], plane_at(-a, -b)
        )
    build(0)
    block_here(4, 4)
    for hop in (1, -1, 3, 2):
        to_chip(4 + hop, hop)
    block_here(-4, -4)
    for hop in (-1, 1, -3, -2):
        to_chip(-4 + hop, hop)
    way = 4 - 8 * core
    far = z_at(-way)
    send(gath.at[far], gath.at[far], z_send.at[15], z_recv.at[15], {"ch": z_at(way)})
    build(1)
    build(-1)
    near_tile = (z + 2) // 4 + 3

    def tile_of(half, n):
        return lax.rem(near_tile + 2 * half + n, 4)

    def spread_out(half):
        largest = None
        for n in range(2):
            filters = gath[pl.ds(tile_of(half, n) * 8, 8)].reshape(128, CELLS)
            sums = lax.dot_general(
                cols[...], filters, (((1,), (1,)), ((), ())), preferred_element_type=F32
            )
            most = jnp.max(jnp.abs(sums), axis=0, keepdims=True)
            largest = most if largest is None else jnp.maximum(largest, most)
            for a in range(SIDE):
                for side in range(2):
                    at = (2 * a + side) * PART
                    part[half, a * SIDE + 2 * n + side] = sums[at : at + PART]
        factor = scale_for(jnp.max(largest, axis=1, keepdims=True))
        for n in range(SIDE * SIDE):
            codes[half, n, :PART, :] = encode(part[half, n], factor.astype(F32))
            codes[half, n, PART:, :] = jnp.broadcast_to(factor, (8, 128))
        for n, (a, b) in enumerate(OTHERS):
            peer = plane_at(a, b)
            send(
                codes.at[half, peer["lat"] * SIDE + peer["lon"]],
                got.at[half, n],
                rs_send.at[half, n],
                rs_recv.at[half, n],
                peer,
            )

    mine_at = lat * SIDE + lon

    def add_up(half):
        share = part[half, mine_at]
        for n, (a, b) in enumerate(OTHERS):
            arrived(got.at[half, n], rs_send.at[half, n], rs_recv.at[half, n], plane_at(-a, -b))
            share += decode(got[half, n])
        share *= scale
        largest = jnp.max(jnp.max(jnp.abs(share), axis=0, keepdims=True), axis=1, keepdims=True)
        factor = scale_for(largest)
        full[half, mine_at, :PART, :] = encode(share, factor.astype(F32))
        full[half, mine_at, PART:, :] = jnp.broadcast_to(factor, (8, 128))
        for n, (a, b) in enumerate(OTHERS):
            send(
                full.at[half, mine_at],
                full.at[half, mine_at],
                ag_send.at[half, n],
                ag_recv.at[half, n],
                plane_at(a, b),
            )

    def put(half, at_lat, at_lon):
        lanes = pl.ds(pl.multiple_of(tile_of(half, at_lon // 2) * 128, 128), 128)
        row = at_lat * 2 * PER + (at_lon % 2) * PER
        value = decode(full[half, at_lat * SIDE + at_lon]).reshape(PER, 8, 128)
        for n in (6, 5):
            wg_ref[pl.ds(jnp.minimum(row + n, TAPS * 2 - 1), 1), :, lanes] = value[n : n + 1]
        wg_ref[pl.ds(row, 5), :, lanes] = value[:5]

    def collect(half):
        put(half, lat, lon)
        for n, (a, b) in enumerate(OTHERS):
            peer = plane_at(-a, -b)
            arrived(
                full.at[half, peer["lat"] * SIDE + peer["lon"]],
                ag_send.at[half, n],
                ag_recv.at[half, n],
                peer,
            )
            put(half, peer["lat"], peer["lon"])

    def sibling_here(dists):
        for dist in dists:
            slot = lax.rem(z - dist + nz, nz) * 2 + (1 - core)
            at = (dist + 7) % 16
            arrived(gath.at[slot], sib_send.at[at], sib_recv.at[at], {"ch": sibling})

    for dist, hop in ((2, 1), (-2, -1), (3, -1), (-3, 1), (5, 1), (-5, -1)):
        block_here(dist, hop)
    sibling_here((0, 1, -1, 4, -4, 2, -2, 3, -3, 5, -5))
    spread_out(0)
    for dist, hop in ((6, 2), (-6, -2), (7, 3), (-7, -3)):
        block_here(dist, hop)
    block_here(8, way)
    sibling_here((6, -6, 7, -7, 8))
    spread_out(1)
    add_up(0)

    fetches[2].wait()
    prod[...] = jnp.dot(
        wts[...].reshape(TAPS * CH, FILT),
        gath[...].reshape(FILT, CELLS),
        preferred_element_type=F32,
    )
    sums = shifted_sums(lambda tap: prod[tap * CH : tap * CH + CH, :], places)
    mine = sums[0, 0]
    lat_out[0] = sums[1, 0][:, 0:256]
    lat_out[1] = sums[-1, 0][:, CELLS - 256 : CELLS]
    columns = [(a, b) for a in (-1, 0, 1) for b in (-1, 1)]
    for n, at in enumerate(columns):
        pt_out[n] = pack_column(sums[at])
    prod[0:CH, :] = mine
    for n, a in enumerate((1, -1)):
        send(lat_out.at[n], lat_in.at[n], ph_send.at[n], ph_recv.at[n], plane_at(a, 0))
    for n, (a, b) in enumerate(columns):
        send(pt_out.at[n], pt_in.at[n], ph_send.at[2 + n], ph_recv.at[2 + n], plane_at(a, b))

    add_up(1)

    for n, a in enumerate((1, -1)):
        arrived(lat_in.at[n], ph_send.at[n], ph_recv.at[n], plane_at(-a, 0))
    for n, (a, b) in enumerate(columns):
        arrived(pt_in.at[n], ph_send.at[2 + n], ph_recv.at[2 + n], plane_at(-a, -b))
    total = prod[0:CH, :]
    total += jnp.concatenate(
        [lat_in[0] * south, jnp.zeros((CH, CELLS - 512), F32), lat_in[1] * north], axis=1
    )
    for n, (a, b) in enumerate(columns):
        packed = pt_in[n]
        if a != 0:
            packed = packed * (south if a == 1 else north)
        total += unpack_column(packed, places, 0 if b == 1 else COLS - 1)
    xg_ref[...] = from_lanes(total.astype(BF16), spread, keep)

    collect(0)
    collect(1)
    for copy in sends:
        copy.wait_send()


def body(inputs, weights, out_grad):
    nz = lax.axis_size("ch") // 2
    cells = CELLS * lax.axis_size("lat") * lax.axis_size("lon")
    dma = pltpu.SemaphoreType.DMA
    vmem = pl.BlockSpec(memory_space=pltpu.VMEM)
    whole = pl.BlockSpec(memory_space=pltpu.HBM)
    input_grad, weight_grad = pl.pallas_call(
        lambda *refs: kernel(nz, 1.0 / math.sqrt(cells), *refs),
        out_shape=(
            jax.ShapeDtypeStruct((CH * GROUPS, COLS), BF16),
            jax.ShapeDtypeStruct((TAPS * 2, 8, FILT), F32),
        ),
        in_specs=[whole] * 3,
        out_specs=(vmem, vmem),
        scratch_shapes=[
            pltpu.VMEM((CH * GROUPS, COLS), BF16),
            pltpu.VMEM((CH * GROUPS, COLS), BF16),
            pltpu.VMEM((9, CH, CELLS), BF16),
            pltpu.VMEM((2 * SIDE * PART, CELLS), BF16),
            pltpu.VMEM((2 * nz, CH, CELLS), BF16),
            pltpu.VMEM((TAPS, CH, FILT), BF16),
            pltpu.VMEM((TAPS * CH, CELLS), F32),
            pltpu.VMEM((2, SIDE * SIDE, PART, 128), F32),
            pltpu.VMEM((2, SIDE * SIDE, PART + 8, 128), BF16),
            pltpu.VMEM((2, 15, PART + 8, 128), BF16),
            pltpu.VMEM((2, SIDE * SIDE, PART + 8, 128), BF16),
            pltpu.VMEM((2, CH, 256), F32),
            pltpu.VMEM((2, CH, 256), F32),
            pltpu.VMEM((6, CH, 128), F32),
            pltpu.VMEM((6, CH, 128), F32),
            dma((3,)),
            dma((16,)),
            dma((16,)),
            dma((16,)),
            dma((16,)),
            dma((8,)),
            dma((8,)),
            dma((8,)),
            dma((8,)),
            dma((2, 15)),
            dma((2, 15)),
            dma((2, 15)),
            dma((2, 15)),
        ],
        compiler_params=pltpu.CompilerParams(
            collective_id=0, has_side_effects=True, vmem_limit_bytes=VMEM_BYTES
        ),
    )(
        *(
            pltpu.with_memory_space_constraint(array, pltpu.HBM)
            for array in (
                inputs.reshape(CH * GROUPS, COLS),
                jnp.transpose(weights, (1, 0, 2)),
                out_grad.reshape(CH * GROUPS, COLS),
            )
        )
    )
    weight_grad = weight_grad.reshape(TAPS, CH, FILT)
    return input_grad.reshape(inputs.shape), jnp.transpose(weight_grad, (1, 0, 2))


def solution(mesh):
    in_specs = (P("ch", None, "lat", "lon"), P("ch", None, None), P("ch", None, "lat", "lon"))
    out_specs = (P("ch", None, "lat", "lon"), P("ch", None, None))
    return jax.shard_map(body, mesh=mesh, in_specs=in_specs, out_specs=out_specs, check_vma=False)
```

```python
import math

import jax
import jax.numpy as jnp
from jax import lax
from jax.experimental import pallas as pl
from jax.experimental.pallas import tpu as pltpu
from jax.sharding import PartitionSpec as P

MESH = pl.DeviceIdType.MESH
F32 = jnp.float32
BF16 = jnp.bfloat16

CH = 16
LEV = 4
ROWS = 4
COLS = 48
GROUPS = ROWS * LEV
CELLS = GROUPS * COLS
SIDE = 4
TAPS = 27
PER = 7
PART = PER * CH // 2
FILT = 512
STEP_LAT = LEV * COLS
TOP = 2.0**30
TINY = 1e-28
VMEM_BYTES = 24 << 20
OTHERS = sorted(
    ((a, b) for a in range(SIDE) for b in range(SIDE) if (a, b) != (0, 0)),
    key=lambda at: -(min(at[0], SIDE - at[0]) + min(at[1], SIDE - at[1])),
)
PIECES = (((0, PART + 8),), ((0, PART + 8),))
ORDER = [(half, piece) for half in range(2) for piece in range(len(PIECES[half]))]
NEAR = [(a, b) for a in (-1, 0, 1) for b in (-1, 0, 1) if (a, b) != (0, 0)]


def roll(values, shift):
    return pltpu.roll(values, shift % values.shape[1], axis=1)


def iota(shape, dim):
    return lax.broadcasted_iota(jnp.int32, shape, dim)


def group_of(lane):
    return lax.shift_right_logical(lane * 1366, 16)


def lane_places(rows):
    lane = iota((rows, CELLS), 1)
    group = group_of(lane)
    return lax.shift_right_logical(group, 2), group & 3, lane - group * COLS


def spread_matrix():
    lane = iota((COLS, CELLS), 1)
    return jnp.where(lane - group_of(lane) * COLS == iota((COLS, CELLS), 0), 1.0, 0.0).astype(BF16)


def keep_matrix():
    row = iota((GROUPS, CELLS), 0)
    group = (row & 3) * 4 + lax.shift_right_logical(row, 2)
    return jnp.where(group_of(iota((GROUPS, CELLS), 1)) == group, 1.0, 0.0).astype(F32)


def to_lanes(block, spread, keep):
    wide = jnp.dot(block, spread, preferred_element_type=F32).reshape(CH, GROUPS, CELLS)
    wide = (wide * keep[None]).reshape(CH * GROUPS, CELLS).astype(BF16)
    shape = (CH, CH * GROUPS)
    pick = jnp.where(lax.shift_right_logical(iota(shape, 1), 4) == iota(shape, 0), 1.0, 0.0).astype(BF16)
    return jnp.dot(pick, wide, preferred_element_type=F32).astype(BF16)


def from_lanes(cells, spread, keep):
    shape = (CH * GROUPS, CH)
    pick = jnp.where(lax.shift_right_logical(iota(shape, 0), 4) == iota(shape, 1), 1.0, 0.0).astype(BF16)
    wide = jnp.dot(pick, cells, preferred_element_type=F32).reshape(CH, GROUPS, CELLS)
    wide = (wide * keep[None]).reshape(CH * GROUPS, CELLS).astype(BF16)
    return lax.dot_general(
        wide, spread, (((1,), (1,)), ((), ())), preferred_element_type=F32
    ).astype(BF16)


def moved_row(near, d_lat, places):
    row, _, _ = places
    moved = {}
    for b in (-1, 0, 1):
        if d_lat == 0:
            moved[b] = near(0, b)
        elif d_lat == 1:
            moved[b] = roll(jnp.where(row == 0, near(1, b), near(0, b)), -STEP_LAT)
        else:
            moved[b] = roll(jnp.where(row == ROWS - 1, near(-1, b), near(0, b)), STEP_LAT)
    return moved


def taps_of_row(moved, places):
    _, level, col = places
    for d_lon in (-1, 0, 1):
        if d_lon == 0:
            base = moved[0]
        elif d_lon == 1:
            base = jnp.where(col == COLS - 1, roll(moved[1], COLS - 1), roll(moved[0], -1))
        else:
            base = jnp.where(col == 0, roll(moved[-1], 1 - COLS), roll(moved[0], 1))
        yield 0, d_lon, base
        yield 1, d_lon, jnp.where(level < LEV - 1, roll(base, -COLS), 0.0)
        yield -1, d_lon, jnp.where(level > 0, roll(base, COLS), 0.0)


def shifted_sums(product, places):
    row, level, col = places
    own = {}
    east = {}
    west = {}
    for d_lat in (-1, 0, 1):
        q = {}
        for d_lon in (-1, 0, 1):
            tap = (d_lat + 1) * 3 + d_lon + 1
            q[d_lon] = (
                product(9 + tap)
                + jnp.where(level > 0, roll(product(18 + tap), COLS), 0.0)
                + jnp.where(level < LEV - 1, roll(product(tap), -COLS), 0.0)
            )
        own[d_lat] = (
            q[0]
            + jnp.where(col > 0, roll(q[1], 1), 0.0)
            + jnp.where(col < COLS - 1, roll(q[-1], -1), 0.0)
        )
        east[d_lat] = jnp.where(col == 0, roll(q[1], 1 - COLS), 0.0)
        west[d_lat] = jnp.where(col == COLS - 1, roll(q[-1], COLS - 1), 0.0)
    out = {}
    for b, sums in ((0, own), (1, east), (-1, west)):
        up = roll(sums[1], STEP_LAT)
        down = roll(sums[-1], -STEP_LAT)
        out[0, b] = (
            sums[0] + jnp.where(row > 0, up, 0.0) + jnp.where(row < ROWS - 1, down, 0.0)
        )
        out[1, b] = jnp.where(row == 0, up, 0.0)
        out[-1, b] = jnp.where(row == ROWS - 1, down, 0.0)
    return out


def pack_column(frame):
    low = frame[:, 0:128] + frame[:, 128:256] + frame[:, 256:384]
    high = frame[:, 384:512] + frame[:, 512:640] + frame[:, 640:768]
    return low + roll(high, 1)


def unpack_column(packed, places, at):
    other = roll(packed, -1)
    wide = jnp.concatenate([packed] * 3 + [other] * 3, axis=1)
    return jnp.where(places[2] == at, wide, 0.0)


def encode(values, scale):
    scaled = values * scale
    square = scaled * scaled
    return (square * scaled * jnp.abs(scaled)).astype(BF16)


def decode(codes, inverse):
    power = codes.astype(F32).reshape(codes.shape[0] // 8, 8, 128)
    root = lax.rsqrt(lax.rsqrt(jnp.abs(power))) * inverse[None]
    return jnp.where(power < 0, -root, root).reshape(codes.shape)


def scale_for(largest):
    return (TOP / jnp.maximum(largest, TINY)).astype(BF16)


def kernel(
    nz,
    scale,
    x_hbm,
    w_hbm,
    g_hbm,
    xg_ref,
    wg_ref,
    x_own,
    g_own,
    field,
    cols,
    gath,
    wts,
    prod,
    part,
    codes,
    got,
    full,
    scales,
    least_of,
    lat_out,
    lat_in,
    pt_out,
    pt_in,
    in_sem,
    z_send,
    z_recv,
    sib_send,
    sib_recv,
    xh_send,
    xh_recv,
    ph_send,
    ph_recv,
    rs_send,
    rs_recv,
    ag_send,
    ag_recv,
):
    ch = lax.axis_index("ch")
    lat = lax.axis_index("lat")
    lon = lax.axis_index("lon")
    z = ch // 2
    core = ch % 2
    sibling = z * 2 + (1 - core)
    here = {"lat": lat, "lon": lon}

    fetches = [
        pltpu.make_async_copy(src, dst, in_sem.at[n])
        for n, (src, dst) in enumerate(((g_hbm, g_own), (x_hbm, x_own), (w_hbm, wts)))
    ]
    for fetch in fetches:
        fetch.start()

    def z_at(step):
        return lax.rem(z + step + nz, nz) * 2 + core

    def side_at(axis, step):
        return lax.rem(here[axis] + step + SIDE, SIDE)

    def plane_at(a, b):
        return {"lat": side_at("lat", a), "lon": side_at("lon", b)}

    barrier = pltpu.get_barrier_semaphore()
    peers = [{"ch": z_at(step)} for step in (4, -4, 3, -3, 2, -2, 1, -1)]
    peers += [{"ch": sibling}] + [plane_at(a, b) for a, b in OTHERS]
    for peer in peers:
        pl.semaphore_signal(barrier, inc=1, device_id=peer, device_id_type=MESH)

    places = lane_places(CH)
    spread = spread_matrix()
    keep = keep_matrix()
    fetches[0].wait()
    gath[ch] = to_lanes(g_own[...], spread, keep)
    fetches[1].wait()
    field[8] = to_lanes(x_own[...], spread, keep)

    pl.semaphore_wait(barrier, len(peers))

    def copy_of(src, dst, send_sem, recv_sem, peer):
        return pltpu.make_async_remote_copy(
            src_ref=src,
            dst_ref=dst,
            send_sem=send_sem,
            recv_sem=recv_sem,
            device_id=peer,
            device_id_type=MESH,
        )

    def send(*args):
        copy_of(*args).start()

    def arrived(dst, sem):
        copy_of(dst, dst, sem, sem, {"ch": sibling}).wait_recv()

    def sent(src, sem):
        copy_of(src, src, sem, sem, {"ch": sibling}).wait_send()

    def to_chip(dist, hop):
        slot = z_at(hop - dist)
        at = (dist + 7) % 16
        send(
            gath.at[slot],
            gath.at[slot],
            z_send,
            z_recv.at[at],
            {"ch": z_at(hop)},
        )

    def to_sibling(dist):
        slot = z_at(-dist)
        late = 0 if abs(dist) <= 5 else 1
        send(gath.at[slot], gath.at[slot], sib_send, sib_recv.at[late], {"ch": sibling})

    def block_here(dist):
        arrived(gath.at[z_at(-dist)], z_recv.at[(dist + 7) % 16])
        to_sibling(dist)

    for dist in (4, -4, 1, -1):
        to_chip(dist, dist)
    to_sibling(0)
    for n, (a, b) in enumerate(NEAR):
        send(field.at[8], field.at[n], xh_send, xh_recv, plane_at(-a, -b))

    south = jnp.where(lat > 0, 1.0, 0.0).astype(F32)
    north = jnp.where(lat < SIDE - 1, 1.0, 0.0).astype(F32)
    inside = {-1: south, 1: north}

    def near(a, b):
        block = field[NEAR.index((a, b)) if (a, b) != (0, 0) else 8].astype(F32)
        return block if a == 0 else block * inside[a]

    def build(d_lat):
        for d_lev, d_lon, value in taps_of_row(moved_row(near, d_lat, places), places):
            tap = (d_lev + 1) * 9 + (d_lat + 1) * 3 + d_lon + 1
            cols[tap * CH : tap * CH + CH, :] = value.astype(BF16)

    cols[TAPS * CH :, :] = jnp.zeros((CH, CELLS), BF16)
    block_here(1)
    to_chip(2, 1)
    block_here(-1)
    to_chip(-2, -1)
    arrived(field.at[pl.ds(0, 8)], xh_recv)
    build(0)
    block_here(4)
    for hop in (3, 2, 1, -1):
        to_chip(4 + hop, hop)
    block_here(-4)
    for hop in (-3, -2, -1, 1):
        to_chip(-4 + hop, hop)
    way = 4 - 8 * core
    far = z_at(-way)
    send(gath.at[far], gath.at[far], z_send, z_recv.at[15], {"ch": z_at(way)})
    build(1)
    build(-1)
    near_tile = (z + 2) // 4 + 3

    def tile_of(half, n):
        return lax.rem(near_tile + 2 * half + n, 4)

    def spread_out(half):
        largest = None
        for n in range(2):
            filters = gath[pl.ds(tile_of(half, n) * 8, 8)].reshape(128, CELLS)
            sums = lax.dot_general(
                cols[...], filters, (((1,), (1,)), ((), ())), preferred_element_type=F32
            )
            most = jnp.max(jnp.abs(sums), axis=0, keepdims=True)
            largest = most if largest is None else jnp.maximum(largest, most)
            for a in range(SIDE):
                for side in range(2):
                    at = (2 * a + side) * PART
                    part[half, a * SIDE + 2 * n + side] = sums[at : at + PART]
        factor = scale_for(jnp.max(largest, axis=1, keepdims=True))
        scales[half] = jnp.broadcast_to(factor, (8, 128)).astype(F32)
        for n, (a, b) in enumerate(OTHERS):
            peer = plane_at(a, b)
            codes[half, n, :8, :] = jnp.broadcast_to(factor, (8, 128))
            codes[half, n, 8:, :] = encode(
                part[half, peer["lat"] * SIDE + peer["lon"]], factor.astype(F32)
            )
        for piece, (start, end) in enumerate(PIECES[half]):
            rows = pl.ds(start, end - start)
            for n, (a, b) in enumerate(OTHERS):
                send(
                    codes.at[half, n, rows],
                    got.at[half, n, rows],
                    rs_send.at[half, piece],
                    rs_recv.at[half, piece],
                    plane_at(a, b),
                )

    mine_at = lat * SIDE + lon

    def add_up(half, piece):
        start, end = PIECES[half][piece]
        rows = pl.ds(start, end - start)
        arrived(got.at[half, pl.ds(0, 15), rows], rs_recv.at[half, piece])
        if piece == 0:
            least = scales[half]
            for n in range(len(OTHERS)):
                least = jnp.minimum(least, got[half, n, :8, :].astype(F32))
            least_of[half] = least
        low, high = max(start - 8, 0), end - 8
        share = part[half, mine_at, low:high]
        for n in range(len(OTHERS)):
            share += decode(
                got[half, n, low + 8 : high + 8, :], 1.0 / got[half, n, :8, :].astype(F32)
            )
        factor = least_of[half] * (1.0 / (SIDE * SIDE))
        share = share.reshape((high - low) // 8, 8, 128)
        full[half, 15, low:high, :] = encode(share, factor[None]).reshape(high - low, 128)
        rows = pl.ds(low, high - low)
        for n, (a, b) in enumerate(OTHERS):
            send(
                full.at[half, 15, rows],
                full.at[half, n, rows],
                ag_send.at[half, piece],
                ag_recv.at[half, piece],
                plane_at(a, b),
            )

    def put(half, piece, n, at_lat, at_lon, inverse):
        start, end = PIECES[half][piece]
        low, high = max(start // 8 - 1, 0), end // 8 - 1
        lanes = pl.ds(pl.multiple_of(tile_of(half, at_lon // 2) * 128, 128), 128)
        row = at_lat * 2 * PER + (at_lon % 2) * PER
        value = decode(full[half, n, low * 8 : high * 8, :], inverse)
        value = value.reshape(high - low, 8, 128)
        for k in range(high - 1, max(low, 5) - 1, -1):
            at = jnp.minimum(row + k, TAPS * 2 - 1)
            wg_ref[pl.ds(at, 1), :, lanes] = value[k - low : k - low + 1]
        for k in range(low, min(high, 5)):
            wg_ref[pl.ds(row + k, 1), :, lanes] = value[k - low : k - low + 1]

    def collect(half, piece):
        start, end = PIECES[half][piece]
        low, high = max(start - 8, 0), end - 8
        inverse = (SIDE * SIDE * scale) / least_of[half]
        put(half, piece, 15, lat, lon, inverse)
        arrived(full.at[half, pl.ds(0, 15), pl.ds(low, high - low)], ag_recv.at[half, piece])
        for n, (a, b) in enumerate(OTHERS):
            peer = plane_at(-a, -b)
            put(half, piece, n, peer["lat"], peer["lon"], inverse)

    for dist in (2, -2, 3, -3, 5, -5):
        block_here(dist)
    arrived(gath.at[pl.ds(0, 11)], sib_recv.at[0])
    spread_out(0)
    for dist in (6, -6, 7, -7, 8):
        block_here(dist)
    arrived(gath.at[pl.ds(0, 5)], sib_recv.at[1])
    spread_out(1)
    sent(field.at[pl.ds(0, 8)], xh_send)
    sent(gath.at[pl.ds(0, 15)], z_send)
    sent(gath.at[pl.ds(0, 16)], sib_send)

    fetches[2].wait()
    prod[...] = jnp.dot(
        wts[...].reshape(TAPS * CH, FILT),
        gath[...].reshape(FILT, CELLS),
        preferred_element_type=F32,
    )
    sums = shifted_sums(lambda tap: prod[tap * CH : tap * CH + CH, :], places)
    mine = sums[0, 0]
    lat_out[0] = sums[1, 0][:, 0:256]
    lat_out[1] = sums[-1, 0][:, CELLS - 256 : CELLS]
    columns = [(a, b) for a in (-1, 0, 1) for b in (-1, 1)]
    for n, at in enumerate(columns):
        pt_out[n] = pack_column(sums[at])
    prod[0:CH, :] = mine
    for n, a in enumerate((1, -1)):
        send(lat_out.at[n], lat_in.at[n], ph_send.at[0], ph_recv.at[0], plane_at(a, 0))
    for n, (a, b) in enumerate(columns):
        send(pt_out.at[n], pt_in.at[n], ph_send.at[1], ph_recv.at[1], plane_at(a, b))

    for half, piece in ORDER:
        add_up(half, piece)

    arrived(lat_in, ph_recv.at[0])
    arrived(pt_in, ph_recv.at[1])
    total = prod[0:CH, :]
    total += jnp.concatenate(
        [lat_in[0] * south, jnp.zeros((CH, CELLS - 512), F32), lat_in[1] * north], axis=1
    )
    for n, (a, b) in enumerate(columns):
        packed = pt_in[n]
        if a != 0:
            packed = packed * (south if a == 1 else north)
        total += unpack_column(packed, places, 0 if b == 1 else COLS - 1)
    xg_ref[...] = from_lanes(total.astype(BF16), spread, keep)

    sent(lat_out, ph_send.at[0])
    sent(pt_out, ph_send.at[1])
    for half, piece in ORDER:
        start, end = PIECES[half][piece]
        sent(codes.at[half, pl.ds(0, 15), pl.ds(start, end - start)], rs_send.at[half, piece])
    for half, piece in ORDER:
        collect(half, piece)
    for half, piece in ORDER:
        start, end = PIECES[half][piece]
        low, high = max(start - 8, 0), end - 8
        sent(full.at[half, pl.ds(0, 15), pl.ds(low, high - low)], ag_send.at[half, piece])


def body(inputs, weights, out_grad):
    nz = lax.axis_size("ch") // 2
    cells = CELLS * lax.axis_size("lat") * lax.axis_size("lon")
    dma = pltpu.SemaphoreType.DMA
    vmem = pl.BlockSpec(memory_space=pltpu.VMEM)
    whole = pl.BlockSpec(memory_space=pltpu.HBM)
    input_grad, weight_grad = pl.pallas_call(
        lambda *refs: kernel(nz, 1.0 / math.sqrt(cells), *refs),
        out_shape=(
            jax.ShapeDtypeStruct((CH * GROUPS, COLS), BF16),
            jax.ShapeDtypeStruct((TAPS * 2, 8, FILT), F32),
        ),
        in_specs=[whole] * 3,
        out_specs=(vmem, vmem),
        scratch_shapes=[
            pltpu.VMEM((CH * GROUPS, COLS), BF16),
            pltpu.VMEM((CH * GROUPS, COLS), BF16),
            pltpu.VMEM((9, CH, CELLS), BF16),
            pltpu.VMEM((2 * SIDE * PART, CELLS), BF16),
            pltpu.VMEM((2 * nz, CH, CELLS), BF16),
            pltpu.VMEM((TAPS, CH, FILT), BF16),
            pltpu.VMEM((TAPS * CH, CELLS), F32),
            pltpu.VMEM((2, SIDE * SIDE, PART, 128), F32),
            pltpu.VMEM((2, 15, PART + 8, 128), BF16),
            pltpu.VMEM((2, 15, PART + 8, 128), BF16),
            pltpu.VMEM((2, SIDE * SIDE, PART, 128), BF16),
            pltpu.VMEM((2, 8, 128), F32),
            pltpu.VMEM((2, 8, 128), F32),
            pltpu.VMEM((2, CH, 256), F32),
            pltpu.VMEM((2, CH, 256), F32),
            pltpu.VMEM((6, CH, 128), F32),
            pltpu.VMEM((6, CH, 128), F32),
            dma((3,)),
            dma,
            dma((16,)),
            dma,
            dma((2,)),
            dma,
            dma,
            dma((2,)),
            dma((2,)),
            dma((2, 2)),
            dma((2, 2)),
            dma((2, 2)),
            dma((2, 2)),
        ],
        compiler_params=pltpu.CompilerParams(
            collective_id=0, has_side_effects=True, vmem_limit_bytes=VMEM_BYTES
        ),
    )(
        *(
            pltpu.with_memory_space_constraint(array, pltpu.HBM)
            for array in (
                inputs.reshape(CH * GROUPS, COLS),
                jnp.transpose(weights, (1, 0, 2)),
                out_grad.reshape(CH * GROUPS, COLS),
            )
        )
    )
    weight_grad = weight_grad.reshape(TAPS, CH, FILT)
    return input_grad.reshape(inputs.shape), jnp.transpose(weight_grad, (1, 0, 2))


def solution(mesh):
    in_specs = (P("ch", None, "lat", "lon"), P("ch", None, None), P("ch", None, "lat", "lon"))
    out_specs = (P("ch", None, "lat", "lon"), P("ch", None, None))
    return jax.shard_map(body, mesh=mesh, in_specs=in_specs, out_specs=out_specs, check_vma=False)
```

```python
import math

import jax
import jax.numpy as jnp
from jax import lax
from jax.experimental import pallas as pl
from jax.experimental.pallas import tpu as pltpu
from jax.sharding import PartitionSpec as P

MESH = pl.DeviceIdType.MESH
F32 = jnp.float32
BF16 = jnp.bfloat16

CH = 16
LEV = 4
ROWS = 4
COLS = 48
GROUPS = ROWS * LEV
CELLS = GROUPS * COLS
SIDE = 4
TAPS = 27
PER = 7
PART = PER * CH // 2
FILT = 512
STEP_LAT = LEV * COLS
TOP = 2.0**30
TINY = 1e-28
VMEM_BYTES = 24 << 20
OTHERS = sorted(
    ((a, b) for a in range(SIDE) for b in range(SIDE) if (a, b) != (0, 0)),
    key=lambda at: -(min(at[0], SIDE - at[0]) + min(at[1], SIDE - at[1])),
)
PIECES = (((0, PART + 8),), ((0, PART + 8),))
ORDER = [(half, piece) for half in range(2) for piece in range(len(PIECES[half]))]
NEAR = [(a, b) for a in (-1, 0, 1) for b in (-1, 0, 1) if (a, b) != (0, 0)]


def roll(values, shift):
    return pltpu.roll(values, shift % values.shape[1], axis=1)


def iota(shape, dim):
    return lax.broadcasted_iota(jnp.int32, shape, dim)


def group_of(lane):
    return lax.shift_right_logical(lane * 1366, 16)


def lane_places(rows):
    lane = iota((rows, CELLS), 1)
    group = group_of(lane)
    return lax.shift_right_logical(group, 2), group & 3, lane - group * COLS


def spread_matrix():
    lane = iota((COLS, CELLS), 1)
    return jnp.where(lane - group_of(lane) * COLS == iota((COLS, CELLS), 0), 1.0, 0.0).astype(BF16)


def keep_matrix():
    row = iota((GROUPS, CELLS), 0)
    group = (row & 3) * 4 + lax.shift_right_logical(row, 2)
    return jnp.where(group_of(iota((GROUPS, CELLS), 1)) == group, 1.0, 0.0).astype(F32)


def to_lanes(block, spread, keep):
    wide = jnp.dot(block, spread, preferred_element_type=F32).reshape(CH, GROUPS, CELLS)
    wide = (wide * keep[None]).reshape(CH * GROUPS, CELLS).astype(BF16)
    shape = (CH, CH * GROUPS)
    pick = jnp.where(lax.shift_right_logical(iota(shape, 1), 4) == iota(shape, 0), 1.0, 0.0).astype(BF16)
    return jnp.dot(pick, wide, preferred_element_type=F32).astype(BF16)


def from_lanes(cells, spread, keep):
    shape = (CH * GROUPS, CH)
    pick = jnp.where(lax.shift_right_logical(iota(shape, 0), 4) == iota(shape, 1), 1.0, 0.0).astype(BF16)
    wide = jnp.dot(pick, cells, preferred_element_type=F32).reshape(CH, GROUPS, CELLS)
    wide = (wide * keep[None]).reshape(CH * GROUPS, CELLS).astype(BF16)
    return lax.dot_general(
        wide, spread, (((1,), (1,)), ((), ())), preferred_element_type=F32
    ).astype(BF16)


def moved_row(near, d_lat, places):
    row, _, _ = places
    moved = {}
    for b in (-1, 0, 1):
        if d_lat == 0:
            moved[b] = near(0, b)
        elif d_lat == 1:
            moved[b] = roll(jnp.where(row == 0, near(1, b), near(0, b)), -STEP_LAT)
        else:
            moved[b] = roll(jnp.where(row == ROWS - 1, near(-1, b), near(0, b)), STEP_LAT)
    return moved


def taps_of_row(moved, places):
    _, level, col = places
    for d_lon in (-1, 0, 1):
        if d_lon == 0:
            base = moved[0]
        elif d_lon == 1:
            base = jnp.where(col == COLS - 1, roll(moved[1], COLS - 1), roll(moved[0], -1))
        else:
            base = jnp.where(col == 0, roll(moved[-1], 1 - COLS), roll(moved[0], 1))
        yield 0, d_lon, base
        yield 1, d_lon, jnp.where(level < LEV - 1, roll(base, -COLS), 0.0)
        yield -1, d_lon, jnp.where(level > 0, roll(base, COLS), 0.0)


def shifted_sums(product, places):
    row, level, col = places
    own = {}
    east = {}
    west = {}
    for d_lat in (-1, 0, 1):
        q = {}
        for d_lon in (-1, 0, 1):
            tap = (d_lat + 1) * 3 + d_lon + 1
            q[d_lon] = (
                product(9 + tap)
                + jnp.where(level > 0, roll(product(18 + tap), COLS), 0.0)
                + jnp.where(level < LEV - 1, roll(product(tap), -COLS), 0.0)
            )
        own[d_lat] = (
            q[0]
            + jnp.where(col > 0, roll(q[1], 1), 0.0)
            + jnp.where(col < COLS - 1, roll(q[-1], -1), 0.0)
        )
        east[d_lat] = jnp.where(col == 0, roll(q[1], 1 - COLS), 0.0)
        west[d_lat] = jnp.where(col == COLS - 1, roll(q[-1], COLS - 1), 0.0)
    out = {}
    for b, sums in ((0, own), (1, east), (-1, west)):
        up = roll(sums[1], STEP_LAT)
        down = roll(sums[-1], -STEP_LAT)
        out[0, b] = (
            sums[0] + jnp.where(row > 0, up, 0.0) + jnp.where(row < ROWS - 1, down, 0.0)
        )
        out[1, b] = jnp.where(row == 0, up, 0.0)
        out[-1, b] = jnp.where(row == ROWS - 1, down, 0.0)
    return out


def pack_column(frame):
    low = frame[:, 0:128] + frame[:, 128:256] + frame[:, 256:384]
    high = frame[:, 384:512] + frame[:, 512:640] + frame[:, 640:768]
    return low + roll(high, 1)


def unpack_column(packed, places, at):
    other = roll(packed, -1)
    wide = jnp.concatenate([packed] * 3 + [other] * 3, axis=1)
    return jnp.where(places[2] == at, wide, 0.0)


def encode(values, scale):
    scaled = values * scale
    square = scaled * scaled
    return (square * scaled * jnp.abs(scaled)).astype(BF16)


def decode(codes, inverse):
    power = codes.astype(F32).reshape(codes.shape[0] // 8, 8, 128)
    root = lax.rsqrt(lax.rsqrt(jnp.abs(power))) * inverse[None]
    return jnp.where(power < 0, -root, root).reshape(codes.shape)


def scale_for(largest):
    return (TOP / jnp.maximum(largest, TINY)).astype(BF16)


def kernel(
    nz,
    scale,
    x_hbm,
    w_hbm,
    g_hbm,
    xg_ref,
    wg_ref,
    x_own,
    g_own,
    field,
    cols,
    gath,
    wts,
    prod,
    part,
    codes,
    got,
    full,
    scales,
    least_of,
    lat_out,
    lat_in,
    pt_out,
    pt_in,
    in_sem,
    z_send,
    z_recv,
    sib_send,
    sib_recv,
    xh_send,
    xh_recv,
    ph_send,
    ph_recv,
    rs_send,
    rs_recv,
    ag_send,
    ag_recv,
):
    ch = lax.axis_index("ch")
    lat = lax.axis_index("lat")
    lon = lax.axis_index("lon")
    z = ch // 2
    core = ch % 2
    sibling = z * 2 + (1 - core)
    here = {"lat": lat, "lon": lon}

    fetches = [
        pltpu.make_async_copy(src, dst, in_sem.at[n])
        for n, (src, dst) in enumerate(((g_hbm, g_own), (x_hbm, x_own), (w_hbm, wts)))
    ]
    for fetch in fetches:
        fetch.start()

    def z_at(step):
        return lax.rem(z + step + nz, nz) * 2 + core

    def side_at(axis, step):
        return lax.rem(here[axis] + step + SIDE, SIDE)

    def plane_at(a, b):
        return {"lat": side_at("lat", a), "lon": side_at("lon", b)}

    barrier = pltpu.get_barrier_semaphore()
    peers = [{"ch": z_at(step)} for step in (4, -4, 3, -3, 2, -2, 1, -1)]
    peers += [{"ch": sibling}] + [plane_at(a, b) for a, b in OTHERS]
    for peer in peers:
        pl.semaphore_signal(barrier, inc=1, device_id=peer, device_id_type=MESH)

    places = lane_places(CH)
    spread = spread_matrix()
    keep = keep_matrix()
    fetches[0].wait()
    gath[ch] = to_lanes(g_own[...], spread, keep)
    fetches[1].wait()
    field[8] = to_lanes(x_own[...], spread, keep)

    pl.semaphore_wait(barrier, len(peers))

    def copy_of(src, dst, send_sem, recv_sem, peer):
        return pltpu.make_async_remote_copy(
            src_ref=src,
            dst_ref=dst,
            send_sem=send_sem,
            recv_sem=recv_sem,
            device_id=peer,
            device_id_type=MESH,
        )

    def send(*args):
        copy_of(*args).start()

    def arrived(dst, sem):
        copy_of(dst, dst, sem, sem, {"ch": sibling}).wait_recv()

    def sent(src, sem):
        copy_of(src, src, sem, sem, {"ch": sibling}).wait_send()

    def to_chip(dist, hop):
        slot = z_at(hop - dist)
        at = (dist + 7) % 16
        send(
            gath.at[slot],
            gath.at[slot],
            z_send,
            z_recv.at[at],
            {"ch": z_at(hop)},
        )

    def to_sibling(dist):
        slot = z_at(-dist)
        late = 0 if abs(dist) <= 5 else 1
        send(gath.at[slot], gath.at[slot], sib_send, sib_recv.at[late], {"ch": sibling})

    def block_here(dist):
        arrived(gath.at[z_at(-dist)], z_recv.at[(dist + 7) % 16])
        to_sibling(dist)

    for dist in (4, -4, 1, -1):
        to_chip(dist, dist)
    to_sibling(0)
    for n, (a, b) in enumerate(NEAR):
        send(field.at[8], field.at[n], xh_send, xh_recv, plane_at(-a, -b))

    south = jnp.where(lat > 0, 1.0, 0.0).astype(F32)
    north = jnp.where(lat < SIDE - 1, 1.0, 0.0).astype(F32)
    inside = {-1: south, 1: north}

    def near(a, b):
        block = field[NEAR.index((a, b)) if (a, b) != (0, 0) else 8].astype(F32)
        return block if a == 0 else block * inside[a]

    def build(d_lat):
        for d_lev, d_lon, value in taps_of_row(moved_row(near, d_lat, places), places):
            tap = (d_lev + 1) * 9 + (d_lat + 1) * 3 + d_lon + 1
            cols[tap * CH : tap * CH + CH, :] = value.astype(BF16)

    cols[TAPS * CH :, :] = jnp.zeros((CH, CELLS), BF16)
    block_here(1)
    to_chip(2, 1)
    block_here(-1)
    to_chip(-2, -1)
    arrived(field.at[pl.ds(0, 8)], xh_recv)
    build(0)
    block_here(4)
    for hop in (3, 1, 2, -1):
        to_chip(4 + hop, hop)
    block_here(-4)
    for hop in (-3, -1, -2, 1):
        to_chip(-4 + hop, hop)
    way = 4 - 8 * core
    far = z_at(-way)
    send(gath.at[far], gath.at[far], z_send, z_recv.at[15], {"ch": z_at(way)})
    build(1)
    build(-1)
    near_tile = (z + 2) // 4 + 3

    def tile_of(half, n):
        return lax.rem(near_tile + 2 * half + n, 4)

    def spread_out(half):
        largest = None
        for n in range(2):
            filters = gath[pl.ds(tile_of(half, n) * 8, 8)].reshape(128, CELLS)
            sums = lax.dot_general(
                cols[...], filters, (((1,), (1,)), ((), ())), preferred_element_type=F32
            )
            most = jnp.max(jnp.abs(sums), axis=0, keepdims=True)
            largest = most if largest is None else jnp.maximum(largest, most)
            for a in range(SIDE):
                for side in range(2):
                    at = (2 * a + side) * PART
                    part[half, a * SIDE + 2 * n + side] = sums[at : at + PART]
        factor = scale_for(jnp.max(largest, axis=1, keepdims=True))
        scales[half] = jnp.broadcast_to(factor, (8, 128)).astype(F32)
        for n, (a, b) in enumerate(OTHERS):
            peer = plane_at(a, b)
            codes[half, n, :8, :] = jnp.broadcast_to(factor, (8, 128))
            codes[half, n, 8:, :] = encode(
                part[half, peer["lat"] * SIDE + peer["lon"]], factor.astype(F32)
            )
        for piece, (start, end) in enumerate(PIECES[half]):
            rows = pl.ds(start, end - start)
            for n, (a, b) in enumerate(OTHERS):
                send(
                    codes.at[half, n, rows],
                    got.at[half, n, rows],
                    rs_send.at[half, piece],
                    rs_recv.at[half, piece],
                    plane_at(a, b),
                )

    mine_at = lat * SIDE + lon

    def add_up(half, piece):
        start, end = PIECES[half][piece]
        rows = pl.ds(start, end - start)
        arrived(got.at[half, pl.ds(0, 15), rows], rs_recv.at[half, piece])
        if piece == 0:
            least = scales[half]
            for n in range(len(OTHERS)):
                least = jnp.minimum(least, got[half, n, :8, :].astype(F32))
            least_of[half] = least
        low, high = max(start - 8, 0), end - 8
        share = part[half, mine_at, low:high]
        for n in range(len(OTHERS)):
            share += decode(
                got[half, n, low + 8 : high + 8, :], 1.0 / got[half, n, :8, :].astype(F32)
            )
        factor = least_of[half] * (1.0 / (SIDE * SIDE))
        share = share.reshape((high - low) // 8, 8, 128)
        full[half, 15, low:high, :] = encode(share, factor[None]).reshape(high - low, 128)
        rows = pl.ds(low, high - low)
        for n, (a, b) in enumerate(OTHERS):
            send(
                full.at[half, 15, rows],
                full.at[half, n, rows],
                ag_send.at[half, piece],
                ag_recv.at[half, piece],
                plane_at(a, b),
            )

    def put(half, piece, n, at_lat, at_lon, inverse):
        start, end = PIECES[half][piece]
        low, high = max(start // 8 - 1, 0), end // 8 - 1
        lanes = pl.ds(pl.multiple_of(tile_of(half, at_lon // 2) * 128, 128), 128)
        row = at_lat * 2 * PER + (at_lon % 2) * PER
        value = decode(full[half, n, low * 8 : high * 8, :], inverse)
        value = value.reshape(high - low, 8, 128)
        for k in range(high - 1, max(low, 5) - 1, -1):
            at = jnp.minimum(row + k, TAPS * 2 - 1)
            wg_ref[pl.ds(at, 1), :, lanes] = value[k - low : k - low + 1]
        for k in range(low, min(high, 5)):
            wg_ref[pl.ds(row + k, 1), :, lanes] = value[k - low : k - low + 1]

    def collect(half, piece):
        start, end = PIECES[half][piece]
        low, high = max(start - 8, 0), end - 8
        inverse = (SIDE * SIDE * scale) / least_of[half]
        put(half, piece, 15, lat, lon, inverse)
        arrived(full.at[half, pl.ds(0, 15), pl.ds(low, high - low)], ag_recv.at[half, piece])
        for n, (a, b) in enumerate(OTHERS):
            peer = plane_at(-a, -b)
            put(half, piece, n, peer["lat"], peer["lon"], inverse)

    for dist in (2, -2, 3, -3, 5, -5):
        block_here(dist)
    arrived(gath.at[pl.ds(0, 11)], sib_recv.at[0])
    spread_out(0)
    for dist in (6, -6, 7, -7, 8):
        block_here(dist)
    arrived(gath.at[pl.ds(0, 5)], sib_recv.at[1])
    spread_out(1)
    sent(field.at[pl.ds(0, 8)], xh_send)
    sent(gath.at[pl.ds(0, 15)], z_send)
    sent(gath.at[pl.ds(0, 16)], sib_send)

    fetches[2].wait()
    prod[...] = jnp.dot(
        wts[...].reshape(TAPS * CH, FILT),
        gath[...].reshape(FILT, CELLS),
        preferred_element_type=F32,
    )
    sums = shifted_sums(lambda tap: prod[tap * CH : tap * CH + CH, :], places)
    mine = sums[0, 0]
    lat_out[0] = sums[1, 0][:, 0:256]
    lat_out[1] = sums[-1, 0][:, CELLS - 256 : CELLS]
    columns = [(a, b) for a in (-1, 0, 1) for b in (-1, 1)]
    for n, at in enumerate(columns):
        pt_out[n] = pack_column(sums[at])
    prod[0:CH, :] = mine
    for n, a in enumerate((1, -1)):
        send(lat_out.at[n], lat_in.at[n], ph_send.at[0], ph_recv.at[0], plane_at(a, 0))
    for n, (a, b) in enumerate(columns):
        send(pt_out.at[n], pt_in.at[n], ph_send.at[1], ph_recv.at[1], plane_at(a, b))

    for half, piece in ORDER:
        add_up(half, piece)

    arrived(lat_in, ph_recv.at[0])
    arrived(pt_in, ph_recv.at[1])
    total = prod[0:CH, :]
    total += jnp.concatenate(
        [lat_in[0] * south, jnp.zeros((CH, CELLS - 512), F32), lat_in[1] * north], axis=1
    )
    for n, (a, b) in enumerate(columns):
        packed = pt_in[n]
        if a != 0:
            packed = packed * (south if a == 1 else north)
        total += unpack_column(packed, places, 0 if b == 1 else COLS - 1)
    xg_ref[...] = from_lanes(total.astype(BF16), spread, keep)

    sent(lat_out, ph_send.at[0])
    sent(pt_out, ph_send.at[1])
    for half, piece in ORDER:
        start, end = PIECES[half][piece]
        sent(codes.at[half, pl.ds(0, 15), pl.ds(start, end - start)], rs_send.at[half, piece])
    for half, piece in ORDER:
        collect(half, piece)
    for half, piece in ORDER:
        start, end = PIECES[half][piece]
        low, high = max(start - 8, 0), end - 8
        sent(full.at[half, pl.ds(0, 15), pl.ds(low, high - low)], ag_send.at[half, piece])


def keep_both(x_ref, w_ref, x_out, w_out, sems):
    copies = [
        pltpu.make_async_copy(w_ref, w_out, sems.at[0]),
        pltpu.make_async_copy(x_ref, x_out, sems.at[1]),
    ]
    for copy in copies:
        copy.start()
    for copy in copies:
        copy.wait()


def body(inputs, weights, out_grad):
    nz = lax.axis_size("ch") // 2
    cells = CELLS * lax.axis_size("lat") * lax.axis_size("lon")
    dma = pltpu.SemaphoreType.DMA
    vmem = pl.BlockSpec(memory_space=pltpu.VMEM)
    whole = pl.BlockSpec(memory_space=pltpu.HBM)
    input_grad, weight_grad = pl.pallas_call(
        lambda *refs: kernel(nz, 1.0 / math.sqrt(cells), *refs),
        out_shape=(
            jax.ShapeDtypeStruct((CH * GROUPS, COLS), BF16),
            jax.ShapeDtypeStruct((TAPS * 2, 8, FILT), F32),
        ),
        in_specs=[whole] * 3,
        out_specs=(vmem, vmem),
        scratch_shapes=[
            pltpu.VMEM((CH * GROUPS, COLS), BF16),
            pltpu.VMEM((CH * GROUPS, COLS), BF16),
            pltpu.VMEM((9, CH, CELLS), BF16),
            pltpu.VMEM((2 * SIDE * PART, CELLS), BF16),
            pltpu.VMEM((2 * nz, CH, CELLS), BF16),
            pltpu.VMEM((TAPS, CH, FILT), BF16),
            pltpu.VMEM((TAPS * CH, CELLS), F32),
            pltpu.VMEM((2, SIDE * SIDE, PART, 128), F32),
            pltpu.VMEM((2, 15, PART + 8, 128), BF16),
            pltpu.VMEM((2, 15, PART + 8, 128), BF16),
            pltpu.VMEM((2, SIDE * SIDE, PART, 128), BF16),
            pltpu.VMEM((2, 8, 128), F32),
            pltpu.VMEM((2, 8, 128), F32),
            pltpu.VMEM((2, CH, 256), F32),
            pltpu.VMEM((2, CH, 256), F32),
            pltpu.VMEM((6, CH, 128), F32),
            pltpu.VMEM((6, CH, 128), F32),
            dma((3,)),
            dma,
            dma((16,)),
            dma,
            dma((2,)),
            dma,
            dma,
            dma((2,)),
            dma((2,)),
            dma((2, 2)),
            dma((2, 2)),
            dma((2, 2)),
            dma((2, 2)),
        ],
        compiler_params=pltpu.CompilerParams(
            collective_id=0, has_side_effects=True, vmem_limit_bytes=VMEM_BYTES
        ),
    )(
        *(
            pltpu.with_memory_space_constraint(array, pltpu.HBM)
            for array in (
                inputs.reshape(CH * GROUPS, COLS),
                jnp.transpose(weights, (1, 0, 2)),
                out_grad.reshape(CH * GROUPS, COLS),
            )
        )
    )
    input_grad, weight_grad = pl.pallas_call(
        keep_both,
        out_shape=(
            jax.ShapeDtypeStruct((CH * GROUPS, COLS), BF16),
            jax.ShapeDtypeStruct((TAPS * 2, 8, FILT), F32),
        ),
        in_specs=[vmem, vmem],
        out_specs=[pl.BlockSpec(memory_space=pl.ANY)] * 2,
        scratch_shapes=[dma((2,))],
        compiler_params=pltpu.CompilerParams(vmem_limit_bytes=4 << 20),
    )(input_grad, weight_grad)
    weight_grad = weight_grad.reshape(TAPS, CH, FILT)
    return input_grad.reshape(inputs.shape), jnp.transpose(weight_grad, (1, 0, 2))


def solution(mesh):
    in_specs = (P("ch", None, "lat", "lon"), P("ch", None, None), P("ch", None, "lat", "lon"))
    out_specs = (P("ch", None, "lat", "lon"), P("ch", None, None))
    return jax.shard_map(body, mesh=mesh, in_specs=in_specs, out_specs=out_specs, check_vma=False)
```

```python
import math

import jax
import jax.numpy as jnp
from jax import lax
from jax.experimental import pallas as pl
from jax.experimental.pallas import tpu as pltpu
from jax.sharding import PartitionSpec as P

MESH = pl.DeviceIdType.MESH
F32 = jnp.float32
BF16 = jnp.bfloat16

CH = 16
LEV = 4
ROWS = 4
COLS = 48
GROUPS = ROWS * LEV
CELLS = GROUPS * COLS
SIDE = 4
TAPS = 27
PER = 7
PART = PER * CH // 2
FILT = 512
STEP_LAT = LEV * COLS
TOP = 2.0**30
TINY = 1e-28
VMEM_BYTES = 24 << 20
OTHERS = sorted(
    ((a, b) for a in range(SIDE) for b in range(SIDE) if (a, b) != (0, 0)),
    key=lambda at: -(min(at[0], SIDE - at[0]) + min(at[1], SIDE - at[1])),
)
PIECES = (((0, PART + 8),), ((0, PART + 8),))
ORDER = [(half, piece) for half in range(2) for piece in range(len(PIECES[half]))]
NEAR = [(a, b) for a in (-1, 0, 1) for b in (-1, 0, 1) if (a, b) != (0, 0)]


def roll(values, shift):
    return pltpu.roll(values, shift % values.shape[1], axis=1)


def iota(shape, dim):
    return lax.broadcasted_iota(jnp.int32, shape, dim)


def group_of(lane):
    return lax.shift_right_logical(lane * 1366, 16)


def lane_places(rows):
    lane = iota((rows, CELLS), 1)
    group = group_of(lane)
    return lax.shift_right_logical(group, 2), group & 3, lane - group * COLS


def spread_matrix():
    lane = iota((COLS, CELLS), 1)
    return jnp.where(lane - group_of(lane) * COLS == iota((COLS, CELLS), 0), 1.0, 0.0).astype(BF16)


def keep_matrix():
    row = iota((GROUPS, CELLS), 0)
    group = (row & 3) * 4 + lax.shift_right_logical(row, 2)
    return jnp.where(group_of(iota((GROUPS, CELLS), 1)) == group, 1.0, 0.0).astype(F32)


def to_lanes(block, spread, keep):
    wide = jnp.dot(block, spread, preferred_element_type=F32).reshape(CH, GROUPS, CELLS)
    wide = (wide * keep[None]).reshape(CH * GROUPS, CELLS).astype(BF16)
    shape = (CH, CH * GROUPS)
    pick = jnp.where(lax.shift_right_logical(iota(shape, 1), 4) == iota(shape, 0), 1.0, 0.0).astype(BF16)
    return jnp.dot(pick, wide, preferred_element_type=F32).astype(BF16)


def from_lanes(cells, spread, keep):
    shape = (CH * GROUPS, CH)
    pick = jnp.where(lax.shift_right_logical(iota(shape, 0), 4) == iota(shape, 1), 1.0, 0.0).astype(BF16)
    wide = jnp.dot(pick, cells, preferred_element_type=F32).reshape(CH, GROUPS, CELLS)
    wide = (wide * keep[None]).reshape(CH * GROUPS, CELLS).astype(BF16)
    return lax.dot_general(
        wide, spread, (((1,), (1,)), ((), ())), preferred_element_type=F32
    ).astype(BF16)


def moved_row(near, d_lat, places):
    row, _, _ = places
    moved = {}
    for b in (-1, 0, 1):
        if d_lat == 0:
            moved[b] = near(0, b)
        elif d_lat == 1:
            moved[b] = roll(jnp.where(row == 0, near(1, b), near(0, b)), -STEP_LAT)
        else:
            moved[b] = roll(jnp.where(row == ROWS - 1, near(-1, b), near(0, b)), STEP_LAT)
    return moved


def taps_of_row(moved, places):
    _, level, col = places
    for d_lon in (-1, 0, 1):
        if d_lon == 0:
            base = moved[0]
        elif d_lon == 1:
            base = jnp.where(col == COLS - 1, roll(moved[1], COLS - 1), roll(moved[0], -1))
        else:
            base = jnp.where(col == 0, roll(moved[-1], 1 - COLS), roll(moved[0], 1))
        yield 0, d_lon, base
        yield 1, d_lon, jnp.where(level < LEV - 1, roll(base, -COLS), 0.0)
        yield -1, d_lon, jnp.where(level > 0, roll(base, COLS), 0.0)


def shifted_sums(product, places):
    row, level, col = places
    own = {}
    east = {}
    west = {}
    for d_lat in (-1, 0, 1):
        q = {}
        for d_lon in (-1, 0, 1):
            tap = (d_lat + 1) * 3 + d_lon + 1
            q[d_lon] = (
                product(9 + tap)
                + jnp.where(level > 0, roll(product(18 + tap), COLS), 0.0)
                + jnp.where(level < LEV - 1, roll(product(tap), -COLS), 0.0)
            )
        own[d_lat] = (
            q[0]
            + jnp.where(col > 0, roll(q[1], 1), 0.0)
            + jnp.where(col < COLS - 1, roll(q[-1], -1), 0.0)
        )
        east[d_lat] = jnp.where(col == 0, roll(q[1], 1 - COLS), 0.0)
        west[d_lat] = jnp.where(col == COLS - 1, roll(q[-1], COLS - 1), 0.0)
    out = {}
    for b, sums in ((0, own), (1, east), (-1, west)):
        up = roll(sums[1], STEP_LAT)
        down = roll(sums[-1], -STEP_LAT)
        out[0, b] = (
            sums[0] + jnp.where(row > 0, up, 0.0) + jnp.where(row < ROWS - 1, down, 0.0)
        )
        out[1, b] = jnp.where(row == 0, up, 0.0)
        out[-1, b] = jnp.where(row == ROWS - 1, down, 0.0)
    return out


def pack_column(frame):
    low = frame[:, 0:128] + frame[:, 128:256] + frame[:, 256:384]
    high = frame[:, 384:512] + frame[:, 512:640] + frame[:, 640:768]
    return low + roll(high, 1)


def unpack_column(packed, places, at):
    other = roll(packed, -1)
    wide = jnp.concatenate([packed] * 3 + [other] * 3, axis=1)
    return jnp.where(places[2] == at, wide, 0.0)


def encode(values, scale):
    scaled = values * scale
    square = scaled * scaled
    return (square * scaled * jnp.abs(scaled)).astype(BF16)


def decode(codes, inverse):
    power = codes.astype(F32).reshape(codes.shape[0] // 8, 8, 128)
    root = lax.rsqrt(lax.rsqrt(jnp.abs(power))) * inverse[None]
    return jnp.where(power < 0, -root, root).reshape(codes.shape)


def scale_for(largest):
    return (TOP / jnp.maximum(largest, TINY)).astype(BF16)


def kernel(
    nz,
    scale,
    x_hbm,
    w_hbm,
    g_hbm,
    xg_ref,
    wg_ref,
    x_own,
    g_own,
    field,
    cols,
    gath,
    wts,
    prod,
    part,
    codes,
    got,
    full,
    scales,
    least_of,
    lat_out,
    lat_in,
    pt_out,
    pt_in,
    in_sem,
    z_send,
    z_recv,
    sib_send,
    sib_recv,
    xh_send,
    xh_recv,
    ph_send,
    ph_recv,
    rs_send,
    rs_recv,
    ag_send,
    ag_recv,
):
    ch = lax.axis_index("ch")
    lat = lax.axis_index("lat")
    lon = lax.axis_index("lon")
    z = ch // 2
    core = ch % 2
    sibling = z * 2 + (1 - core)
    here = {"lat": lat, "lon": lon}

    known = {}

    def z_at(step):
        if not isinstance(step, int):
            return lax.rem(z + step + nz, nz) * 2 + core
        if step not in known:
            known[step] = lax.rem(z + step + nz, nz) * 2 + core
        return known[step]

    def side_at(axis, step):
        step = step % SIDE
        if step == 0:
            return here[axis]
        if (axis, step) not in known:
            known[axis, step] = lax.rem(here[axis] + step, SIDE)
        return known[axis, step]

    def plane_at(a, b):
        return {"lat": side_at("lat", a), "lon": side_at("lon", b)}

    def whole(peer):
        return peer.get("ch", ch), peer.get("lat", lat), peer.get("lon", lon)

    barrier = pltpu.get_barrier_semaphore()
    peers = [{"ch": z_at(step)} for step in (4, -4, 3, -3, 2, -2, 1, -1)]
    peers += [{"ch": sibling}] + [plane_at(a, b) for a, b in OTHERS]
    for peer in peers:
        pl.semaphore_signal(barrier, inc=1, device_id=whole(peer), device_id_type=MESH)

    fetches = [
        pltpu.make_async_copy(src, dst, in_sem.at[n])
        for n, (src, dst) in enumerate(((g_hbm, g_own), (x_hbm, x_own), (w_hbm, wts)))
    ]
    for fetch in fetches:
        fetch.start()

    places = lane_places(CH)
    spread = spread_matrix()
    keep = keep_matrix()
    fetches[0].wait()
    gath[ch] = to_lanes(g_own[...], spread, keep)
    fetches[1].wait()
    field[8] = to_lanes(x_own[...], spread, keep)

    pl.semaphore_wait(barrier, len(peers))

    def copy_of(src, dst, send_sem, recv_sem, peer):
        return pltpu.make_async_remote_copy(
            src_ref=src,
            dst_ref=dst,
            send_sem=send_sem,
            recv_sem=recv_sem,
            device_id=whole(peer),
            device_id_type=MESH,
        )

    def send(*args):
        copy_of(*args).start()

    def arrived(dst, sem):
        copy_of(dst, dst, sem, sem, {"ch": sibling}).wait_recv()

    def sent(src, sem):
        copy_of(src, src, sem, sem, {"ch": sibling}).wait_send()

    def to_chip(dist, hop):
        slot = z_at(hop - dist)
        at = (dist + 7) % 16
        send(
            gath.at[slot],
            gath.at[slot],
            z_send,
            z_recv.at[at],
            {"ch": z_at(hop)},
        )

    def to_sibling(dist):
        slot = z_at(-dist)
        late = 0 if abs(dist) <= 5 else 1
        send(gath.at[slot], gath.at[slot], sib_send, sib_recv.at[late], {"ch": sibling})

    def block_here(dist, hops=()):
        arrived(gath.at[z_at(-dist)], z_recv.at[(dist + 7) % 16])
        for hop in hops:
            to_chip(dist + hop, hop)
        to_sibling(dist)

    for dist in (4, -4, 1, -1):
        to_chip(dist, dist)
    to_sibling(0)
    for n, (a, b) in enumerate(NEAR):
        send(field.at[8], field.at[n], xh_send, xh_recv, plane_at(-a, -b))

    south = jnp.where(lat > 0, 1.0, 0.0).astype(F32)
    north = jnp.where(lat < SIDE - 1, 1.0, 0.0).astype(F32)
    inside = {-1: south, 1: north}

    def near(a, b):
        block = field[NEAR.index((a, b)) if (a, b) != (0, 0) else 8].astype(F32)
        return block if a == 0 else block * inside[a]

    def build(d_lat):
        for d_lev, d_lon, value in taps_of_row(moved_row(near, d_lat, places), places):
            tap = (d_lev + 1) * 9 + (d_lat + 1) * 3 + d_lon + 1
            cols[tap * CH : tap * CH + CH, :] = value.astype(BF16)

    cols[TAPS * CH :, :] = jnp.zeros((CH, CELLS), BF16)
    block_here(1, (1,))
    block_here(-1, (-1,))
    arrived(field.at[pl.ds(0, 8)], xh_recv)
    build(0)
    block_here(4, (3, 1, 2, -1))
    block_here(-4, (-3, -1, -2, 1))
    way = 4 - 8 * core
    far = z_at(-way)
    send(gath.at[far], gath.at[far], z_send, z_recv.at[15], {"ch": z_at(way)})
    build(1)
    build(-1)
    near_tile = (z + 2) // 4 + 3

    def tile_of(half, n):
        return lax.rem(near_tile + 2 * half + n, 4)

    def spread_out(half):
        filters = jnp.concatenate(
            [gath[pl.ds(tile_of(half, n) * 8, 8)].reshape(128, CELLS) for n in range(2)], axis=0
        )
        both = lax.dot_general(
            cols[...], filters, (((1,), (1,)), ((), ())), preferred_element_type=F32
        )
        largest = jnp.max(jnp.abs(both), axis=0, keepdims=True)
        for n in range(2):
            sums = both[:, n * 128 : n * 128 + 128]
            for a in range(SIDE):
                for side in range(2):
                    at = (2 * a + side) * PART
                    part[half, a * SIDE + 2 * n + side] = sums[at : at + PART]
        factor = scale_for(jnp.max(largest, axis=1, keepdims=True))
        scales[half] = jnp.broadcast_to(factor, (8, 128)).astype(F32)
        for n, (a, b) in enumerate(OTHERS):
            peer = plane_at(a, b)
            codes[half, n, :8, :] = jnp.broadcast_to(factor, (8, 128))
            codes[half, n, 8:, :] = encode(
                part[half, peer["lat"] * SIDE + peer["lon"]], factor.astype(F32)
            )
        for piece, (start, end) in enumerate(PIECES[half]):
            rows = pl.ds(start, end - start)
            for n, (a, b) in enumerate(OTHERS):
                send(
                    codes.at[half, n, rows],
                    got.at[half, n, rows],
                    rs_send.at[half, piece],
                    rs_recv.at[half, piece],
                    plane_at(a, b),
                )

    mine_at = lat * SIDE + lon

    def add_up(half, piece):
        start, end = PIECES[half][piece]
        rows = pl.ds(start, end - start)
        arrived(got.at[half, pl.ds(0, 15), rows], rs_recv.at[half, piece])
        if piece == 0:
            least = scales[half]
            for n in range(len(OTHERS)):
                least = jnp.minimum(least, got[half, n, :8, :].astype(F32))
            least_of[half] = least
        low, high = max(start - 8, 0), end - 8
        share = part[half, mine_at, low:high]
        for n in range(len(OTHERS)):
            share += decode(
                got[half, n, low + 8 : high + 8, :], 1.0 / got[half, n, :8, :].astype(F32)
            )
        factor = least_of[half] * (1.0 / (SIDE * SIDE))
        share = share.reshape((high - low) // 8, 8, 128)
        full[half, 15, low:high, :] = encode(share, factor[None]).reshape(high - low, 128)
        rows = pl.ds(low, high - low)
        for n, (a, b) in enumerate(OTHERS):
            send(
                full.at[half, 15, rows],
                full.at[half, n, rows],
                ag_send.at[half, piece],
                ag_recv.at[half, piece],
                plane_at(a, b),
            )

    def put(half, piece, n, at_lat, at_lon, inverse):
        start, end = PIECES[half][piece]
        low, high = max(start // 8 - 1, 0), end // 8 - 1
        lanes = pl.ds(pl.multiple_of(tile_of(half, at_lon // 2) * 128, 128), 128)
        row = at_lat * 2 * PER + (at_lon % 2) * PER
        value = decode(full[half, n, low * 8 : high * 8, :], inverse)
        value = value.reshape(high - low, 8, 128)
        for k in range(high - 1, max(low, 5) - 1, -1):
            at = jnp.minimum(row + k, TAPS * 2 - 1)
            wg_ref[pl.ds(at, 1), :, lanes] = value[k - low : k - low + 1]
        for k in range(low, min(high, 5)):
            wg_ref[pl.ds(row + k, 1), :, lanes] = value[k - low : k - low + 1]

    def collect(half, piece):
        start, end = PIECES[half][piece]
        low, high = max(start - 8, 0), end - 8
        inverse = (SIDE * SIDE * scale) / least_of[half]
        put(half, piece, 15, lat, lon, inverse)
        arrived(full.at[half, pl.ds(0, 15), pl.ds(low, high - low)], ag_recv.at[half, piece])
        for n, (a, b) in enumerate(OTHERS):
            peer = plane_at(-a, -b)
            put(half, piece, n, peer["lat"], peer["lon"], inverse)

    for dist in (2, -2, 3, -3, 5, -5):
        block_here(dist)
    arrived(gath.at[pl.ds(0, 11)], sib_recv.at[0])
    spread_out(0)
    for dist in (6, -6, 7, -7, 8):
        block_here(dist)
    arrived(gath.at[pl.ds(0, 5)], sib_recv.at[1])
    spread_out(1)
    sent(field.at[pl.ds(0, 8)], xh_send)
    sent(gath.at[pl.ds(0, 15)], z_send)
    sent(gath.at[pl.ds(0, 16)], sib_send)

    fetches[2].wait()
    prod[...] = jnp.dot(
        wts[...].reshape(TAPS * CH, FILT),
        gath[...].reshape(FILT, CELLS),
        preferred_element_type=F32,
    )
    sums = shifted_sums(lambda tap: prod[tap * CH : tap * CH + CH, :], places)
    mine = sums[0, 0]
    lat_out[0] = sums[1, 0][:, 0:256]
    lat_out[1] = sums[-1, 0][:, CELLS - 256 : CELLS]
    columns = [(a, b) for a in (-1, 0, 1) for b in (-1, 1)]
    for n, at in enumerate(columns):
        pt_out[n] = pack_column(sums[at])
    prod[0:CH, :] = mine
    for n, a in enumerate((1, -1)):
        send(lat_out.at[n], lat_in.at[n], ph_send.at[0], ph_recv.at[0], plane_at(a, 0))
    for n, (a, b) in enumerate(columns):
        send(pt_out.at[n], pt_in.at[n], ph_send.at[1], ph_recv.at[1], plane_at(a, b))

    for half, piece in ORDER:
        add_up(half, piece)

    arrived(lat_in, ph_recv.at[0])
    arrived(pt_in, ph_recv.at[1])
    total = prod[0:CH, :]
    total += jnp.concatenate(
        [lat_in[0] * south, jnp.zeros((CH, CELLS - 512), F32), lat_in[1] * north], axis=1
    )
    for n, (a, b) in enumerate(columns):
        packed = pt_in[n]
        if a != 0:
            packed = packed * (south if a == 1 else north)
        total += unpack_column(packed, places, 0 if b == 1 else COLS - 1)
    xg_ref[...] = from_lanes(total.astype(BF16), spread, keep)

    sent(lat_out, ph_send.at[0])
    sent(pt_out, ph_send.at[1])
    for half, piece in ORDER:
        start, end = PIECES[half][piece]
        sent(codes.at[half, pl.ds(0, 15), pl.ds(start, end - start)], rs_send.at[half, piece])
    for half, piece in ORDER:
        collect(half, piece)
    for half, piece in ORDER:
        start, end = PIECES[half][piece]
        low, high = max(start - 8, 0), end - 8
        sent(full.at[half, pl.ds(0, 15), pl.ds(low, high - low)], ag_send.at[half, piece])


def keep_both(x_ref, w_ref, x_out, w_out, sems):
    copies = [
        pltpu.make_async_copy(w_ref, w_out, sems.at[0]),
        pltpu.make_async_copy(x_ref, x_out, sems.at[1]),
    ]
    for copy in copies:
        copy.start()
    for copy in copies:
        copy.wait()


def body(inputs, weights, out_grad):
    nz = lax.axis_size("ch") // 2
    cells = CELLS * lax.axis_size("lat") * lax.axis_size("lon")
    dma = pltpu.SemaphoreType.DMA
    vmem = pl.BlockSpec(memory_space=pltpu.VMEM)
    whole = pl.BlockSpec(memory_space=pltpu.HBM)
    input_grad, weight_grad = pl.pallas_call(
        lambda *refs: kernel(nz, 1.0 / math.sqrt(cells), *refs),
        out_shape=(
            jax.ShapeDtypeStruct((CH * GROUPS, COLS), BF16),
            jax.ShapeDtypeStruct((TAPS * 2, 8, FILT), F32),
        ),
        in_specs=[whole] * 3,
        out_specs=(vmem, vmem),
        scratch_shapes=[
            pltpu.VMEM((CH * GROUPS, COLS), BF16),
            pltpu.VMEM((CH * GROUPS, COLS), BF16),
            pltpu.VMEM((9, CH, CELLS), BF16),
            pltpu.VMEM((2 * SIDE * PART, CELLS), BF16),
            pltpu.VMEM((2 * nz, CH, CELLS), BF16),
            pltpu.VMEM((TAPS, CH, FILT), BF16),
            pltpu.VMEM((TAPS * CH, CELLS), F32),
            pltpu.VMEM((2, SIDE * SIDE, PART, 128), F32),
            pltpu.VMEM((2, 15, PART + 8, 128), BF16),
            pltpu.VMEM((2, 15, PART + 8, 128), BF16),
            pltpu.VMEM((2, SIDE * SIDE, PART, 128), BF16),
            pltpu.VMEM((2, 8, 128), F32),
            pltpu.VMEM((2, 8, 128), F32),
            pltpu.VMEM((2, CH, 256), F32),
            pltpu.VMEM((2, CH, 256), F32),
            pltpu.VMEM((6, CH, 128), F32),
            pltpu.VMEM((6, CH, 128), F32),
            dma((3,)),
            dma,
            dma((16,)),
            dma,
            dma((2,)),
            dma,
            dma,
            dma((2,)),
            dma((2,)),
            dma((2, 2)),
            dma((2, 2)),
            dma((2, 2)),
            dma((2, 2)),
        ],
        compiler_params=pltpu.CompilerParams(
            collective_id=0, has_side_effects=True, vmem_limit_bytes=VMEM_BYTES
        ),
    )(
        *(
            pltpu.with_memory_space_constraint(array, pltpu.HBM)
            for array in (
                inputs.reshape(CH * GROUPS, COLS),
                jnp.transpose(weights, (1, 0, 2)),
                out_grad.reshape(CH * GROUPS, COLS),
            )
        )
    )
    input_grad, weight_grad = pl.pallas_call(
        keep_both,
        out_shape=(
            jax.ShapeDtypeStruct((CH * GROUPS, COLS), BF16),
            jax.ShapeDtypeStruct((TAPS * 2, 8, FILT), F32),
        ),
        in_specs=[vmem, vmem],
        out_specs=[pl.BlockSpec(memory_space=pl.ANY)] * 2,
        scratch_shapes=[dma((2,))],
        compiler_params=pltpu.CompilerParams(vmem_limit_bytes=4 << 20),
    )(input_grad, weight_grad)
    weight_grad = weight_grad.reshape(TAPS, CH, FILT)
    return input_grad.reshape(inputs.shape), jnp.transpose(weight_grad, (1, 0, 2))


def solution(mesh):
    in_specs = (P("ch", None, "lat", "lon"), P("ch", None, None), P("ch", None, "lat", "lon"))
    out_specs = (P("ch", None, "lat", "lon"), P("ch", None, None))
    return jax.shard_map(body, mesh=mesh, in_specs=in_specs, out_specs=out_specs, check_vma=False)
```

```python
import math

import jax
import jax.numpy as jnp
from jax import lax
from jax.experimental import pallas as pl
from jax.experimental.pallas import tpu as pltpu
from jax.sharding import PartitionSpec as P

MESH = pl.DeviceIdType.MESH
F32 = jnp.float32
BF16 = jnp.bfloat16

CH = 16
LEV = 4
ROWS = 4
COLS = 48
GROUPS = ROWS * LEV
CELLS = GROUPS * COLS
SIDE = 4
TAPS = 27
PER = 7
PART = PER * CH // 2
FILT = 512
STEP_LAT = LEV * COLS
TOP = 2.0**30
TINY = 1e-28
VMEM_BYTES = 24 << 20
OTHERS = [(2, 2), (1, 2), (2, 3), (3, 2), (2, 1), (1, 1), (3, 3), (1, 3), (3, 1), (0, 2), (2, 0), (0, 1), (1, 0), (0, 3), (3, 0)]
PIECES = (((0, PART + 8),), ((0, PART + 8),))
ORDER = [(half, piece) for half in range(2) for piece in range(len(PIECES[half]))]
NEAR = [(a, b) for a in (-1, 0, 1) for b in (-1, 0, 1) if (a, b) != (0, 0)]


def roll(values, shift):
    return pltpu.roll(values, shift % values.shape[1], axis=1)


def iota(shape, dim):
    return lax.broadcasted_iota(jnp.int32, shape, dim)


def group_of(lane):
    return lax.shift_right_logical(lane * 1366, 16)


def lane_places(rows):
    lane = iota((rows, CELLS), 1)
    group = group_of(lane)
    return lax.shift_right_logical(group, 2), group & 3, lane - group * COLS


def spread_matrix():
    lane = iota((COLS, CELLS), 1)
    return jnp.where(lane - group_of(lane) * COLS == iota((COLS, CELLS), 0), 1.0, 0.0).astype(BF16)


def keep_matrix():
    row = iota((GROUPS, CELLS), 0)
    group = (row & 3) * 4 + lax.shift_right_logical(row, 2)
    return jnp.where(group_of(iota((GROUPS, CELLS), 1)) == group, 1.0, 0.0).astype(F32)


def to_lanes(block, spread, keep):
    wide = jnp.dot(block, spread, preferred_element_type=F32).reshape(CH, GROUPS, CELLS)
    wide = (wide * keep[None]).reshape(CH * GROUPS, CELLS).astype(BF16)
    shape = (CH, CH * GROUPS)
    pick = jnp.where(lax.shift_right_logical(iota(shape, 1), 4) == iota(shape, 0), 1.0, 0.0).astype(BF16)
    return jnp.dot(pick, wide, preferred_element_type=F32).astype(BF16)


def from_lanes(cells, spread, keep):
    shape = (CH * GROUPS, CH)
    pick = jnp.where(lax.shift_right_logical(iota(shape, 0), 4) == iota(shape, 1), 1.0, 0.0).astype(BF16)
    wide = jnp.dot(pick, cells, preferred_element_type=F32).reshape(CH, GROUPS, CELLS)
    wide = (wide * keep[None]).reshape(CH * GROUPS, CELLS).astype(BF16)
    return lax.dot_general(
        wide, spread, (((1,), (1,)), ((), ())), preferred_element_type=F32
    ).astype(BF16)


def moved_row(near, d_lat, places):
    row, _, _ = places
    moved = {}
    for b in (-1, 0, 1):
        if d_lat == 0:
            moved[b] = near(0, b)
        elif d_lat == 1:
            moved[b] = roll(jnp.where(row == 0, near(1, b), near(0, b)), -STEP_LAT)
        else:
            moved[b] = roll(jnp.where(row == ROWS - 1, near(-1, b), near(0, b)), STEP_LAT)
    return moved


def taps_of_row(moved, places):
    _, level, col = places
    for d_lon in (-1, 0, 1):
        if d_lon == 0:
            base = moved[0]
        elif d_lon == 1:
            base = jnp.where(col == COLS - 1, roll(moved[1], COLS - 1), roll(moved[0], -1))
        else:
            base = jnp.where(col == 0, roll(moved[-1], 1 - COLS), roll(moved[0], 1))
        yield 0, d_lon, base
        yield 1, d_lon, jnp.where(level < LEV - 1, roll(base, -COLS), 0.0)
        yield -1, d_lon, jnp.where(level > 0, roll(base, COLS), 0.0)


def shifted_sums(product, places):
    row, level, col = places
    own = {}
    east = {}
    west = {}
    for d_lat in (-1, 0, 1):
        q = {}
        for d_lon in (-1, 0, 1):
            tap = (d_lat + 1) * 3 + d_lon + 1
            q[d_lon] = (
                product(9 + tap)
                + jnp.where(level > 0, roll(product(18 + tap), COLS), 0.0)
                + jnp.where(level < LEV - 1, roll(product(tap), -COLS), 0.0)
            )
        own[d_lat] = (
            q[0]
            + jnp.where(col > 0, roll(q[1], 1), 0.0)
            + jnp.where(col < COLS - 1, roll(q[-1], -1), 0.0)
        )
        east[d_lat] = jnp.where(col == 0, roll(q[1], 1 - COLS), 0.0)
        west[d_lat] = jnp.where(col == COLS - 1, roll(q[-1], COLS - 1), 0.0)
    out = {}
    for b, sums in ((0, own), (1, east), (-1, west)):
        up = roll(sums[1], STEP_LAT)
        down = roll(sums[-1], -STEP_LAT)
        out[0, b] = (
            sums[0] + jnp.where(row > 0, up, 0.0) + jnp.where(row < ROWS - 1, down, 0.0)
        )
        out[1, b] = jnp.where(row == 0, up, 0.0)
        out[-1, b] = jnp.where(row == ROWS - 1, down, 0.0)
    return out


def pack_column(frame):
    low = frame[:, 0:128] + frame[:, 128:256] + frame[:, 256:384]
    high = frame[:, 384:512] + frame[:, 512:640] + frame[:, 640:768]
    return low + roll(high, 1)


def unpack_column(packed, places, at):
    other = roll(packed, -1)
    wide = jnp.concatenate([packed] * 3 + [other] * 3, axis=1)
    return jnp.where(places[2] == at, wide, 0.0)


def encode(values, scale):
    scaled = values * scale
    square = scaled * scaled
    return (square * scaled * jnp.abs(scaled)).astype(BF16)


def decode(codes, inverse):
    power = codes.astype(F32).reshape(codes.shape[0] // 8, 8, 128)
    root = lax.rsqrt(lax.rsqrt(jnp.abs(power))) * inverse[None]
    return jnp.where(power < 0, -root, root).reshape(codes.shape)


def scale_for(largest):
    return (TOP / jnp.maximum(largest, TINY)).astype(BF16)


def kernel(
    nz,
    scale,
    x_hbm,
    w_hbm,
    g_hbm,
    xg_ref,
    wg_ref,
    x_own,
    g_own,
    field,
    cols,
    gath,
    wts,
    prod,
    part,
    codes,
    got,
    full,
    scales,
    least_of,
    lat_out,
    lat_in,
    pt_out,
    pt_in,
    in_sem,
    z_send,
    z_recv,
    sib_send,
    sib_recv,
    xh_send,
    xh_recv,
    ph_send,
    ph_recv,
    rs_send,
    rs_recv,
    ag_send,
    ag_recv,
):
    ch = lax.axis_index("ch")
    lat = lax.axis_index("lat")
    lon = lax.axis_index("lon")
    z = ch // 2
    core = ch % 2
    sibling = z * 2 + (1 - core)
    here = {"lat": lat, "lon": lon}

    known = {}

    def z_at(step):
        if not isinstance(step, int):
            return lax.rem(z + step + nz, nz) * 2 + core
        if step not in known:
            known[step] = lax.rem(z + step + nz, nz) * 2 + core
        return known[step]

    def side_at(axis, step):
        step = step % SIDE
        if step == 0:
            return here[axis]
        if (axis, step) not in known:
            known[axis, step] = lax.rem(here[axis] + step, SIDE)
        return known[axis, step]

    def plane_at(a, b):
        return {"lat": side_at("lat", a), "lon": side_at("lon", b)}

    def whole(peer):
        return peer.get("ch", ch), peer.get("lat", lat), peer.get("lon", lon)

    barrier = pltpu.get_barrier_semaphore()
    peers = [{"ch": z_at(step)} for step in (4, -4, 3, -3, 2, -2, 1, -1)]
    peers += [{"ch": sibling}] + [plane_at(a, b) for a, b in OTHERS]
    for peer in peers:
        pl.semaphore_signal(barrier, inc=1, device_id=whole(peer), device_id_type=MESH)

    fetches = [
        pltpu.make_async_copy(src, dst, in_sem.at[n])
        for n, (src, dst) in enumerate(((g_hbm, g_own), (x_hbm, x_own), (w_hbm, wts)))
    ]
    for fetch in fetches:
        fetch.start()

    places = lane_places(CH)
    spread = spread_matrix()
    keep = keep_matrix()
    fetches[0].wait()
    gath[ch] = to_lanes(g_own[...], spread, keep)
    fetches[1].wait()
    field[8] = to_lanes(x_own[...], spread, keep)

    pl.semaphore_wait(barrier, len(peers))

    def copy_of(src, dst, send_sem, recv_sem, peer):
        return pltpu.make_async_remote_copy(
            src_ref=src,
            dst_ref=dst,
            send_sem=send_sem,
            recv_sem=recv_sem,
            device_id=whole(peer),
            device_id_type=MESH,
        )

    def send(*args):
        copy_of(*args).start()

    def arrived(dst, sem):
        copy_of(dst, dst, sem, sem, {"ch": sibling}).wait_recv()

    def sent(src, sem):
        copy_of(src, src, sem, sem, {"ch": sibling}).wait_send()

    def to_chip(dist, hop):
        slot = z_at(hop - dist)
        at = (dist + 7) % 16
        send(
            gath.at[slot],
            gath.at[slot],
            z_send,
            z_recv.at[at],
            {"ch": z_at(hop)},
        )

    def to_sibling(dist):
        slot = z_at(-dist)
        late = 0 if abs(dist) <= 5 else 1
        send(gath.at[slot], gath.at[slot], sib_send, sib_recv.at[late], {"ch": sibling})

    def block_here(dist, hops=()):
        arrived(gath.at[z_at(-dist)], z_recv.at[(dist + 7) % 16])
        for hop in hops:
            to_chip(dist + hop, hop)
        to_sibling(dist)

    for dist in (4, -4, 1, -1):
        to_chip(dist, dist)
    to_sibling(0)
    for n, (a, b) in enumerate(NEAR):
        send(field.at[8], field.at[n], xh_send, xh_recv, plane_at(-a, -b))

    south = jnp.where(lat > 0, 1.0, 0.0).astype(F32)
    north = jnp.where(lat < SIDE - 1, 1.0, 0.0).astype(F32)
    inside = {-1: south, 1: north}

    def near(a, b):
        block = field[NEAR.index((a, b)) if (a, b) != (0, 0) else 8].astype(F32)
        return block if a == 0 else block * inside[a]

    def build(d_lat):
        for d_lev, d_lon, value in taps_of_row(moved_row(near, d_lat, places), places):
            tap = (d_lev + 1) * 9 + (d_lat + 1) * 3 + d_lon + 1
            cols[tap * CH : tap * CH + CH, :] = value.astype(BF16)

    cols[TAPS * CH :, :] = jnp.zeros((CH, CELLS), BF16)
    block_here(1, (1,))
    block_here(-1, (-1,))
    arrived(field.at[pl.ds(0, 8)], xh_recv)
    build(0)
    block_here(4, (3, 1, 2, -1))
    block_here(-4, (-3, -1, -2, 1))
    way = 4 - 8 * core
    far = z_at(-way)
    send(gath.at[far], gath.at[far], z_send, z_recv.at[15], {"ch": z_at(way)})
    build(1)
    build(-1)
    near_tile = (z + 2) // 4 + 3

    def tile_of(half, n):
        return lax.rem(near_tile + 2 * half + n, 4)

    def spread_out(half):
        filters = jnp.concatenate(
            [gath[pl.ds(tile_of(half, n) * 8, 8)].reshape(128, CELLS) for n in range(2)], axis=0
        )
        both = lax.dot_general(
            cols[...], filters, (((1,), (1,)), ((), ())), preferred_element_type=F32
        )
        largest = jnp.max(jnp.abs(both), axis=0, keepdims=True)
        for n in range(2):
            sums = both[:, n * 128 : n * 128 + 128]
            for a in range(SIDE):
                for side in range(2):
                    at = (2 * a + side) * PART
                    part[half, a * SIDE + 2 * n + side] = sums[at : at + PART]
        factor = scale_for(jnp.max(largest, axis=1, keepdims=True))
        scales[half] = jnp.broadcast_to(factor, (8, 128)).astype(F32)
        for n, (a, b) in enumerate(OTHERS):
            peer = plane_at(a, b)
            codes[half, n, :8, :] = jnp.broadcast_to(factor, (8, 128))
            codes[half, n, 8:, :] = encode(
                part[half, peer["lat"] * SIDE + peer["lon"]], factor.astype(F32)
            )
        for piece, (start, end) in enumerate(PIECES[half]):
            rows = pl.ds(start, end - start)
            for n, (a, b) in enumerate(OTHERS):
                send(
                    codes.at[half, n, rows],
                    got.at[half, n, rows],
                    rs_send.at[half, piece],
                    rs_recv.at[half, piece],
                    plane_at(a, b),
                )

    mine_at = lat * SIDE + lon

    def add_up(half, piece):
        start, end = PIECES[half][piece]
        rows = pl.ds(start, end - start)
        arrived(got.at[half, pl.ds(0, 15), rows], rs_recv.at[half, piece])
        if piece == 0:
            least = scales[half]
            for n in range(len(OTHERS)):
                least = jnp.minimum(least, got[half, n, :8, :].astype(F32))
            least_of[half] = least
        low, high = max(start - 8, 0), end - 8
        share = part[half, mine_at, low:high]
        for n in range(len(OTHERS)):
            share += decode(
                got[half, n, low + 8 : high + 8, :], 1.0 / got[half, n, :8, :].astype(F32)
            )
        factor = least_of[half] * (1.0 / (SIDE * SIDE))
        share = share.reshape((high - low) // 8, 8, 128)
        full[half, 15, low:high, :] = encode(share, factor[None]).reshape(high - low, 128)
        rows = pl.ds(low, high - low)
        for n, (a, b) in enumerate(OTHERS):
            send(
                full.at[half, 15, rows],
                full.at[half, n, rows],
                ag_send.at[half, piece],
                ag_recv.at[half, piece],
                plane_at(a, b),
            )

    def put(half, piece, n, at_lat, at_lon, inverse):
        start, end = PIECES[half][piece]
        low, high = max(start // 8 - 1, 0), end // 8 - 1
        lanes = pl.ds(pl.multiple_of(tile_of(half, at_lon // 2) * 128, 128), 128)
        row = at_lat * 2 * PER + (at_lon % 2) * PER
        value = decode(full[half, n, low * 8 : high * 8, :], inverse)
        value = value.reshape(high - low, 8, 128)
        for k in range(high - 1, max(low, 5) - 1, -1):
            at = jnp.minimum(row + k, TAPS * 2 - 1)
            wg_ref[pl.ds(at, 1), :, lanes] = value[k - low : k - low + 1]
        for k in range(low, min(high, 5)):
            wg_ref[pl.ds(row + k, 1), :, lanes] = value[k - low : k - low + 1]

    def collect(half, piece):
        start, end = PIECES[half][piece]
        low, high = max(start - 8, 0), end - 8
        inverse = (SIDE * SIDE * scale) / least_of[half]
        put(half, piece, 15, lat, lon, inverse)
        arrived(full.at[half, pl.ds(0, 15), pl.ds(low, high - low)], ag_recv.at[half, piece])
        for n, (a, b) in enumerate(OTHERS):
            peer = plane_at(-a, -b)
            put(half, piece, n, peer["lat"], peer["lon"], inverse)

    for dist in (2, -2, 3, -3, 5, -5):
        block_here(dist)
    arrived(gath.at[pl.ds(0, 11)], sib_recv.at[0])
    spread_out(0)
    for dist in (6, -6, 7, -7, 8):
        block_here(dist)
    arrived(gath.at[pl.ds(0, 5)], sib_recv.at[1])
    spread_out(1)
    sent(field.at[pl.ds(0, 8)], xh_send)
    sent(gath.at[pl.ds(0, 15)], z_send)
    sent(gath.at[pl.ds(0, 16)], sib_send)

    fetches[2].wait()
    prod[...] = jnp.dot(
        wts[...].reshape(TAPS * CH, FILT),
        gath[...].reshape(FILT, CELLS),
        preferred_element_type=F32,
    )
    sums = shifted_sums(lambda tap: prod[tap * CH : tap * CH + CH, :], places)
    mine = sums[0, 0]
    lat_out[0] = sums[1, 0][:, 0:256]
    lat_out[1] = sums[-1, 0][:, CELLS - 256 : CELLS]
    columns = [(a, b) for a in (-1, 0, 1) for b in (-1, 1)]
    for n, at in enumerate(columns):
        pt_out[n] = pack_column(sums[at])
    prod[0:CH, :] = mine
    for n, a in enumerate((1, -1)):
        send(lat_out.at[n], lat_in.at[n], ph_send.at[0], ph_recv.at[0], plane_at(a, 0))
    for n, (a, b) in enumerate(columns):
        send(pt_out.at[n], pt_in.at[n], ph_send.at[1], ph_recv.at[1], plane_at(a, b))

    for half, piece in ORDER:
        add_up(half, piece)

    arrived(lat_in, ph_recv.at[0])
    arrived(pt_in, ph_recv.at[1])
    total = prod[0:CH, :]
    total += jnp.concatenate(
        [lat_in[0] * south, jnp.zeros((CH, CELLS - 512), F32), lat_in[1] * north], axis=1
    )
    for n, (a, b) in enumerate(columns):
        packed = pt_in[n]
        if a != 0:
            packed = packed * (south if a == 1 else north)
        total += unpack_column(packed, places, 0 if b == 1 else COLS - 1)
    xg_ref[...] = from_lanes(total.astype(BF16), spread, keep)

    sent(lat_out, ph_send.at[0])
    sent(pt_out, ph_send.at[1])
    for half, piece in ORDER:
        start, end = PIECES[half][piece]
        sent(codes.at[half, pl.ds(0, 15), pl.ds(start, end - start)], rs_send.at[half, piece])
    for half, piece in ORDER:
        collect(half, piece)
    for half, piece in ORDER:
        start, end = PIECES[half][piece]
        low, high = max(start - 8, 0), end - 8
        sent(full.at[half, pl.ds(0, 15), pl.ds(low, high - low)], ag_send.at[half, piece])


def keep_both(x_ref, w_ref, x_out, w_out, sems):
    copies = [
        pltpu.make_async_copy(w_ref, w_out, sems.at[0]),
        pltpu.make_async_copy(x_ref, x_out, sems.at[1]),
    ]
    for copy in copies:
        copy.start()
    for copy in copies:
        copy.wait()


def body(inputs, weights, out_grad):
    nz = lax.axis_size("ch") // 2
    cells = CELLS * lax.axis_size("lat") * lax.axis_size("lon")
    dma = pltpu.SemaphoreType.DMA
    vmem = pl.BlockSpec(memory_space=pltpu.VMEM)
    whole = pl.BlockSpec(memory_space=pltpu.HBM)
    input_grad, weight_grad = pl.pallas_call(
        lambda *refs: kernel(nz, 1.0 / math.sqrt(cells), *refs),
        out_shape=(
            jax.ShapeDtypeStruct((CH * GROUPS, COLS), BF16),
            jax.ShapeDtypeStruct((TAPS * 2, 8, FILT), F32),
        ),
        in_specs=[whole] * 3,
        out_specs=(vmem, vmem),
        scratch_shapes=[
            pltpu.VMEM((CH * GROUPS, COLS), BF16),
            pltpu.VMEM((CH * GROUPS, COLS), BF16),
            pltpu.VMEM((9, CH, CELLS), BF16),
            pltpu.VMEM((2 * SIDE * PART, CELLS), BF16),
            pltpu.VMEM((2 * nz, CH, CELLS), BF16),
            pltpu.VMEM((TAPS, CH, FILT), BF16),
            pltpu.VMEM((TAPS * CH, CELLS), F32),
            pltpu.VMEM((2, SIDE * SIDE, PART, 128), F32),
            pltpu.VMEM((2, 15, PART + 8, 128), BF16),
            pltpu.VMEM((2, 15, PART + 8, 128), BF16),
            pltpu.VMEM((2, SIDE * SIDE, PART, 128), BF16),
            pltpu.VMEM((2, 8, 128), F32),
            pltpu.VMEM((2, 8, 128), F32),
            pltpu.VMEM((2, CH, 256), F32),
            pltpu.VMEM((2, CH, 256), F32),
            pltpu.VMEM((6, CH, 128), F32),
            pltpu.VMEM((6, CH, 128), F32),
            dma((3,)),
            dma,
            dma((16,)),
            dma,
            dma((2,)),
            dma,
            dma,
            dma((2,)),
            dma((2,)),
            dma((2, 2)),
            dma((2, 2)),
            dma((2, 2)),
            dma((2, 2)),
        ],
        compiler_params=pltpu.CompilerParams(
            collective_id=0, has_side_effects=True, vmem_limit_bytes=VMEM_BYTES
        ),
    )(
        *(
            pltpu.with_memory_space_constraint(array, pltpu.HBM)
            for array in (
                inputs.reshape(CH * GROUPS, COLS),
                jnp.transpose(weights, (1, 0, 2)),
                out_grad.reshape(CH * GROUPS, COLS),
            )
        )
    )
    input_grad, weight_grad = pl.pallas_call(
        keep_both,
        out_shape=(
            jax.ShapeDtypeStruct((CH * GROUPS, COLS), BF16),
            jax.ShapeDtypeStruct((TAPS * 2, 8, FILT), F32),
        ),
        in_specs=[vmem, vmem],
        out_specs=[pl.BlockSpec(memory_space=pl.ANY)] * 2,
        scratch_shapes=[dma((2,))],
        compiler_params=pltpu.CompilerParams(vmem_limit_bytes=4 << 20),
    )(input_grad, weight_grad)
    weight_grad = weight_grad.reshape(TAPS, CH, FILT)
    return input_grad.reshape(inputs.shape), jnp.transpose(weight_grad, (1, 0, 2))


def solution(mesh):
    in_specs = (P("ch", None, "lat", "lon"), P("ch", None, None), P("ch", None, "lat", "lon"))
    out_specs = (P("ch", None, "lat", "lon"), P("ch", None, None))
    return jax.shard_map(body, mesh=mesh, in_specs=in_specs, out_specs=out_specs, check_vma=False)
```
